256 devices in a mesh: dp: 64 (over x, z, y_lo), mp: 4 (over y_hi, core).
Axes of the slice: x: 4, y: 4 (y_hi: 2, y_lo: 2; y = y_hi * 2 + y_lo), z: 8, core: 2. Of those that a mesh axis runs over, the one named last changes fastest.
Arguments:
- cell_states: bfloat16 [16384, 4096], P('dp', 'mp'), may hold values from -6 to 6
- projection: bfloat16 [4096, 1024], P('mp'), may hold values from -0.0029296875 to 0.0029296875
- text_embeds: bfloat16 [16384, 1024], P(('dp', 'mp')), may hold values from -0.1875 to 0.1875
- group_ids: int32 [16384], P('dp'), may hold values from 0 to 2047
Outputs:
- cell_grad: float32 [16384, 1024], P('dp', 'mp')
- text_grad: float32 [16384, 1024], P(('dp', 'mp'))
The draws below stay inside these ranges and needn't reach their ends.
Inputs may be any that keep to these rules, and one draw needn't show every extreme that they name: `group_ids`: a cell and a caption form a positive pair exactly where their ids are equal.
All inputs are finite; a program needn't handle non-finite values.
Results may differ from the reference program's by a relative error of at most 0.0051.
Values may be sent and summed in bfloat16 or wider, within the bound.
A program may use at most 128 MiB of HBM per device.

```python
import jax
import jax.numpy as jnp
from jax import lax

D = 4096
EMB = 1024
BATCH = 16384
GROUPS = 2048
N_DP = 64


def plant(result, key, smallest, largest):
    dims = result.shape
    index_at = [jax.random.randint(jax.random.fold_in(key, axis), (), 0, dims[axis]) for axis in range(len(dims))]
    result = result.at[tuple(index_at)].set(smallest)
    longest = dims.index(max(dims))
    index_at[longest] = (index_at[longest] + 1) % dims[longest]
    return result.at[tuple(index_at)].set(largest)


def block_levels(rng, extent, shards, smallest, high):
    factor_of = 1.0
    for dim, blocks in shards:
        steps = jax.random.uniform(jax.random.fold_in(jax.random.fold_in(rng, 6), dim), (blocks,), jnp.float32, smallest / len(shards), high / len(shards))
        factor_of = factor_of * jnp.repeat(jnp.exp(steps), extent[dim] // blocks).reshape((-1,) + (1,) * (len(extent) - 1 - dim))
    return factor_of


def noise(stream_key, dims, width, limit, cuts=(), held_as=jnp.bfloat16):
    values = width * jax.random.normal(stream_key, dims, jnp.float32)
    if cuts:
        values = values * block_levels(stream_key, dims, cuts, -0.22, 0.18)
    return jnp.clip(values, -limit, limit).astype(held_as)


def setup_inputs(seed: int = 0) -> dict:
    arg_keys = jax.random.split(jax.random.key(seed), 5)
    return {
        "cell_states": noise(arg_keys[0], (BATCH, D), 1.0, 6.0, ((0, 64), (1, 4))),
        "projection": noise(arg_keys[1], (D, EMB), (D * EMB) ** -0.5, 0.0029296875, ((0, 4),)),
        "text_embeds": noise(arg_keys[2], (BATCH, EMB), EMB ** -0.5, 0.1875, ((0, 256),)),
        "group_ids": plant(jax.random.randint(arg_keys[3], (BATCH,), 0, GROUPS), jax.random.fold_in(arg_keys[3], 1), 0, GROUPS - 1).astype(jnp.int32),
    }


logit_scale = 10.0
logit_bias = -4.0
epsilon = 1e-06

def unit_rows(values):
    row_norm = jnp.sqrt(lax.optimization_barrier(jnp.sum(values * values, axis=1)) + epsilon)
    return (values / row_norm[:, None], row_norm)

def rounded(values):
    half = lax.optimization_barrier(values.astype(jnp.bfloat16))
    return half.astype(jnp.float32)

def reference(cell_states, projection, text_embeds, group_ids):
    embedded = jnp.dot(cell_states, projection, preferred_element_type=jnp.float32)
    cell_unit, cell_norm = unit_rows(embedded)
    cell_half = rounded(cell_unit)
    text_unit, text_norm = unit_rows(text_embeds.astype(jnp.float32))
    text_half = rounded(text_unit)
    total_rows = text_half.shape[0]
    width_emb = text_half.shape[1]
    span_rows = min(512, total_rows)
    blocks = total_rows // span_rows
    text_blocks = text_half.reshape(blocks, span_rows, width_emb)
    id_blocks = group_ids.reshape(blocks, span_rows)
    cell_groups = cell_half.reshape(N_DP, total_rows // N_DP, width_emb)

    def visit_block(running, payload):
        text_block, text_ids = payload
        logits = logit_scale * jnp.dot(cell_half, text_block.T, precision=lax.Precision.HIGHEST) + logit_bias
        labels = jnp.where(group_ids[:, None] == text_ids[None, :], 1.0, -1.0).astype(jnp.float32)
        slopes = rounded(-logit_scale * labels * jax.nn.sigmoid(-labels * logits))
        running = running + jnp.dot(slopes, text_block, precision=lax.Precision.HIGHEST)
        slope_groups = slopes.reshape(N_DP, total_rows // N_DP, span_rows)
        parts = jnp.einsum('gis,gie->gse', slope_groups, cell_groups, precision=lax.Precision.HIGHEST)
        return (running, lax.optimization_barrier(jnp.sum(rounded(parts), axis=0)))
    start_pull = jnp.zeros(cell_unit.shape, jnp.float32)
    cell_pull, text_parts = lax.scan(visit_block, start_pull, (text_blocks, id_blocks))
    text_pull = text_parts.reshape(total_rows, width_emb)
    radial = lax.optimization_barrier(jnp.sum(cell_unit * cell_pull, axis=1))
    cell_grad = (cell_pull - cell_unit * radial[:, None]) / cell_norm[:, None]
    text_radial = lax.optimization_barrier(jnp.sum(text_unit * text_pull, axis=1))
    text_grad = (text_pull - text_unit * text_radial[:, None]) / text_norm[:, None]
    return (cell_grad, text_grad)
```

```python
import jax
import jax.numpy as jnp
from jax import lax
from jax.experimental import pallas as pl
from jax.experimental.pallas import tpu as pltpu
from jax.sharding import PartitionSpec as P

MESH = pl.DeviceIdType.MESH
F32, BF16, I32 = jnp.float32, jnp.bfloat16, jnp.int32
WIDE = 1024
EPS = 1e-06
COPIES = 104


class Wire:
    def __init__(self, send, recv):
        self.send, self.recv, self.open = send, recv, []

    def __call__(self, src, dst, where):
        i = len(self.open)
        copy = pltpu.make_async_remote_copy(
            src_ref=src,
            dst_ref=dst,
            send_sem=self.send.at[i],
            recv_sem=self.recv.at[i],
            device_id=where,
            device_id_type=MESH,
        )
        copy.start()
        self.open.append(copy)
        return copy

    def drain(self):
        for copy in self.open:
            copy.wait_send()


def dot(a, b, dims):
    return lax.dot_general(a, b, (dims, ((), ())), preferred_element_type=F32)


def placed(row, start, place, width):
    shift = lax.rem(place - start + 128, 128) // 32
    moved = row
    for k in range(1, 4):
        moved = jnp.where(shift == k, jnp.roll(row, 32 * k, axis=1), moved)
    lane = lax.broadcasted_iota(I32, row.shape, 1)
    return jnp.where((lane >= place) & (lane < place + width), moved, 0)


def ring4(wire, part, stage, got, p, ahead, behind):
    o, n, b = lax.rem(p + 2, 4), lax.rem(p + 1, 4), lax.rem(p + 3, 4)

    def put(q, half, add=None):
        v = part[q, half]
        if add is not None:
            v = v + got[add].astype(F32)
        stage[q, half] = v.astype(BF16)
        return stage.at[q, half]

    f0 = wire(put(o, 0), got.at[0, 0], ahead)
    b0 = wire(put(o, 1), got.at[1, 0], behind)
    f1 = wire(put(n, 1), got.at[0, 1], ahead)
    b1 = wire(put(b, 0), got.at[1, 1], behind)
    yield
    f0.wait_recv()
    f2 = wire(put(n, 0, (0, 0)), got.at[0, 2], ahead)
    b0.wait_recv()
    b2 = wire(put(b, 1, (1, 0)), got.at[1, 2], behind)
    yield
    b1.wait_recv()
    f2.wait_recv()
    low = part[p, 0] + got[0, 2].astype(F32) + got[1, 1].astype(F32)
    f1.wait_recv()
    b2.wait_recv()
    high = part[p, 1] + got[0, 1].astype(F32) + got[1, 2].astype(F32)
    return low, high


def finish(run):
    try:
        next(run)
    except StopIteration as end:
        return end.value


def kernel(
    cs, pj, te, ids, cg, tg,
    T, TI, CC, CI, CU, CN, PS, PO, PR, RU, RD, FN, QS,
    IDR, IDC, SL, CP, XS, XR, ZW, ZR,
    TP, W1, R1, S2, W2, R2, GS, GR, GY, HU, HD, HF,
    send, recv,
):
    dp, mp = lax.axis_index("dp"), lax.axis_index("mp")
    x, z, ylo = dp // 16, lax.rem(dp // 2, 8), lax.rem(dp, 2)
    hi, c = mp // 2, lax.rem(mp, 2)
    y = hi * 2 + ylo

    def dev(x, y, z, c):
        return ((x * 8 + z) * 2 + lax.rem(y, 2), (y // 2) * 2 + c)

    xr, xl = lax.rem(x + 1, 4), lax.rem(x + 3, 4)
    yu, yd = lax.rem(y + 1, 4), lax.rem(y + 3, 4)
    right, left = dev(xr, y, z, c), dev(xl, y, z, c)
    up, down = dev(x, yu, z, c), dev(x, yd, z, c)
    front, back = dev(x, y, lax.rem(z + 1, 8), c), dev(x, y, lax.rem(z + 7, 8), c)
    twin = dev(x, y, z, 1 - c)

    barrier = pltpu.get_barrier_semaphore()
    for where in (right, left, up, down, front, back, twin):
        pl.semaphore_signal(barrier, inc=1, device_id=where, device_id_type=MESH)
    pl.semaphore_wait(barrier, 7)
    wire = Wire(send, recv)

    def zat(k):
        return lax.rem(z + k + 8, 8)

    row = jnp.where(hi == 0, ids[0:1, :], ids[1:2, :])
    TI[y, x, 0:1, :] = placed(row, c * 64, x * 32, 32)
    TI[y, x, 1:2, :] = placed(row, c * 64 + 32, y * 32, 32)
    TI[y, x, 2:8, :] = jnp.zeros((6, 128), I32)
    CI[z] = jnp.broadcast_to(row, (8, 128))
    i_r = wire(TI.at[y, x], TI.at[y, x], right)
    i_l = wire(TI.at[y, x], TI.at[y, x], left)
    c_f = [wire(CI.at[z], CI.at[z], front)]
    c_b = [wire(CI.at[z], CI.at[z], back)]

    def project(core, out):
        rows = cs[:, core].reshape(128, WIDE)
        for n in range(4):
            cols = pl.ds(n * 256, 256)
            out[:, :, cols] = dot(rows, pj[:, cols], ((1,), (0,))).reshape(2, 64, 256)

    project(1 - c, PS)
    p_x = wire(PS, PR, twin)

    text = te[...].astype(F32)
    text_norm = jnp.sqrt(jnp.sum(text * text, axis=1, keepdims=True) + EPS)
    half = (text / text_norm).astype(BF16)
    T[y, x] = half[0:32]
    T[4 + x, y] = half[32:64]
    a_r = wire(T.at[y, x], T.at[y, x], right)
    a_l = wire(T.at[y, x], T.at[y, x], left)
    b_u = wire(T.at[4 + x, y], T.at[4 + x, y], up)
    b_d = wire(T.at[4 + x, y], T.at[4 + x, y], down)

    project(c, PO)
    p_x.wait_recv()
    PO[...] = PO[...] + PR[...]
    QS[...] = PO[1 - hi]
    q_u = wire(QS.at[pl.ds(0, 32)], RU, up)
    q_d = wire(QS.at[pl.ds(32, 32)], RD, down)

    low, high = pl.ds(0, 16), pl.ds(16, 16)
    a_r.wait_recv()
    a_rr = wire(T.at[y, xl, low], T.at[y, xl, low], right)
    a_l.wait_recv()
    a_ll = wire(T.at[y, xr, high], T.at[y, xr, high], left)
    b_u.wait_recv()
    b_uu = wire(T.at[4 + x, yd, low], T.at[4 + x, yd, low], up)
    b_d.wait_recv()
    b_dd = wire(T.at[4 + x, yu, high], T.at[4 + x, yu, high], down)
    i_r.wait_recv()
    i_rr = wire(TI.at[y, xl], TI.at[y, xl], right)
    i_l.wait_recv()
    for k in range(1, 4):
        c_f[-1].wait_recv()
        c_f.append(wire(CI.at[zat(-k)], CI.at[zat(-k)], front))
        c_b[-1].wait_recv()
        if k < 3:
            c_b.append(wire(CI.at[zat(k)], CI.at[zat(k)], back))

    q_u.wait_recv()
    q_uu = wire(RU, FN.at[pl.ds(0, 32)], up)
    q_d.wait_recv()
    q_dd = wire(RD, FN.at[pl.ds(32, 32)], down)

    a_rr.wait_recv()
    a_ll.wait_recv()
    b_uu.wait_recv()
    b_dd.wait_recv()
    i_rr.wait_recv()
    j_u = wire(TI.at[y], TI.at[y], up)
    j_d = wire(TI.at[y], TI.at[y], down)
    b_r = wire(T.at[4 + x], T.at[4 + x], right)
    b_l = wire(T.at[4 + x], T.at[4 + x], left)
    a_u = wire(T.at[y], T.at[y], up)
    a_d = wire(T.at[y], T.at[y], down)

    q_uu.wait_recv()
    q_dd.wait_recv()
    emb = PO[hi] + FN[...]
    cell_norm = jnp.sqrt(jnp.sum(emb * emb, axis=1, keepdims=True) + EPS)
    unit = emb / cell_norm
    CU[...] = unit
    CN[...] = jnp.broadcast_to(cell_norm, (64, 128))
    CC[z, c] = unit.astype(BF16)
    g_f = [wire(CC.at[z, c], CC.at[z, c], front)]
    g_b = [wire(CC.at[z, c], CC.at[z, c], back)]
    g_t = [wire(CC.at[z, c], CC.at[z, c], twin)]

    j_u.wait_recv()
    j_uu = wire(TI.at[yd], TI.at[yd], up)
    j_d.wait_recv()
    first, second = pl.ds(0, 2), pl.ds(2, 2)
    b_r.wait_recv()
    b_rr = wire(T.at[4 + xl, first], T.at[4 + xl, first], right)
    b_l.wait_recv()
    b_ll = wire(T.at[4 + xr, second], T.at[4 + xr, second], left)
    a_u.wait_recv()
    a_uu = wire(T.at[yd, first], T.at[yd, first], up)
    a_d.wait_recv()
    a_dd = wire(T.at[yu, second], T.at[yu, second], down)

    for k in range(1, 5):
        f, b = zat(-k), zat(k)
        g_f[-1].wait_recv()
        g_b[-1].wait_recv()
        if k < 3:
            g_f.append(wire(CC.at[f, c], CC.at[f, c], front))
            g_b.append(wire(CC.at[b, c], CC.at[b, c], back))
        elif k == 3:
            h0, h1 = pl.ds(0, 32), pl.ds(32, 32)
            g_f.append(wire(CC.at[f, c, h0], CC.at[f, c, h0], front))
            g_b.append(wire(CC.at[b, c, h1], CC.at[b, c, h1], back))
        g_t.append(wire(CC.at[f, c], CC.at[f, c], twin))
        if k < 4:
            g_t.append(wire(CC.at[b, c], CC.at[b, c], twin))

    j_uu.wait_recv()
    for k in range(4):
        IDR[k] = sum(TI[k, i, 0:1, :] for i in range(4)).astype(F32)
        IDR[4 + k] = sum(TI[i, k, 1:2, :] for i in range(4)).astype(F32)
    c_f[-1].wait_recv()
    for k in range(8):
        IDC[k * 128 : (k + 1) * 128, :] = jnp.broadcast_to(CI[k, 0:1, :].astype(F32), (128, 128)).T

    for copy in (b_rr, b_ll, a_uu, a_dd, *g_t):
        copy.wait_recv()

    @pl.loop(0, 4)
    def _(t):
        texts = T[pl.ds(t * 2, 2)].reshape(256, WIDE)
        names = jnp.concatenate([IDR[t * 2], IDR[t * 2 + 1]], axis=1)
        for m in range(4):
            cells = CC[2 * m : 2 * m + 2].reshape(256, WIDE)
            inner = dot(cells, texts, ((1,), (1,)))
            col = IDC[m * 256 : (m + 1) * 256, :]
            same = jnp.concatenate([col, col], axis=1) == names
            slope = 5.0 * jnp.tanh(5.0 * inner - 2.0) + jnp.where(same, -5.0, 5.0)
            SL[t, m * 256 : (m + 1) * 256, :] = slope.astype(BF16)

    @pl.loop(0, 4)
    def _(m):
        rows = pl.ds(pl.multiple_of(m * 256, 256), 256)
        total = dot(
            jnp.concatenate([SL[t, rows, :] for t in range(4)], axis=1),
            T[...].reshape(WIDE, WIDE),
            ((1,), (0,)),
        )
        CP[pl.ds(2 * m, 2)] = total.reshape(2, 2, 2, 32, WIDE)

    for k in range(8):
        XS[k] = CP[k, 1 - c].astype(BF16)
    x_t = wire(XS, XR, twin)

    @pl.loop(0, 4)
    def _(t):
        total = dot(SL[t], CC[...].reshape(WIDE, WIDE), ((0,), (0,)))
        TP[pl.ds(2 * t, 2)] = total.reshape(2, 2, 64, WIDE)

    x_t.wait_recv()

    def zput(k, half, add=None):
        q = zat(k)
        v = CP[q, c, half] + XR[q, half].astype(F32)
        if add is not None:
            v = v + ZR[add].astype(F32)
        ZW[q, half] = v.astype(BF16)
        return ZW.at[q, half]

    z_f = [wire(zput(4, 0), ZR.at[0, 0, 0], front)]
    z_b = [wire(zput(-4, 1), ZR.at[1, 0, 1], back)]
    run_a = ring4(wire, TP.at[pl.ds(0, 4)], W1.at[pl.ds(0, 4)], R1.at[0], y, up, down)
    run_b = ring4(wire, TP.at[pl.ds(4, 4)], W1.at[pl.ds(4, 4)], R1.at[1], x, right, left)
    next(run_a)
    next(run_b)
    z_f3 = wire(zput(3, 1), ZR.at[0, 1, 1], front)
    z_b3 = wire(zput(-3, 0), ZR.at[1, 1, 0], back)
    z_f[0].wait_recv()
    z_f = [wire(zput(3, 0, (0, 0, 0)), ZR.at[0, 1, 0], front), z_f3]
    z_b[0].wait_recv()
    z_b = [z_b3, wire(zput(-3, 1, (1, 0, 1)), ZR.at[1, 1, 1], back)]
    next(run_a)
    next(run_b)

    def zstep(k, z_f, z_b):
        f, b = [], []
        for half in range(2):
            z_f[half].wait_recv()
            f.append(wire(zput(4 - k, half, (0, k - 1, half)), ZR.at[0, k, half], front))
            z_b[half].wait_recv()
            b.append(wire(zput(k - 4, half, (1, k - 1, half)), ZR.at[1, k, half], back))
        return f, b

    z_f, z_b = zstep(2, z_f, z_b)
    for h, run in ((0, run_a), (1, run_b)):
        first, second = finish(run)
        S2[h * 4 : h * 4 + 2] = first.reshape(2, 2, 16, WIDE)
        S2[h * 4 + 2 : h * 4 + 4] = second.reshape(2, 2, 16, WIDE)
    run_a = ring4(wire, S2.at[pl.ds(0, 4)], W2.at[pl.ds(0, 4)], R2.at[0], x, right, left)
    run_b = ring4(wire, S2.at[pl.ds(4, 4)], W2.at[pl.ds(4, 4)], R2.at[1], y, up, down)
    next(run_a)
    next(run_b)
    z_f, z_b = zstep(3, z_f, z_b)
    next(run_a)
    next(run_b)

    for copy in (*z_f, *z_b):
        copy.wait_recv()
    pull = (
        CP[z, c].reshape(64, WIDE)
        + XR[z].astype(F32).reshape(64, WIDE)
        + ZR[0, 3].astype(F32).reshape(64, WIDE)
        + ZR[1, 3].astype(F32).reshape(64, WIDE)
    )
    unit = CU[...]
    radial = jnp.sum(unit * pull, axis=1, keepdims=True)
    grad = (pull - unit * radial) / CN[:, 0:1]
    for h in range(2):
        for k in range(2):
            GS[k, h] = grad[:, (h * 2 + k) * 256 : (h * 2 + k + 1) * 256]
    o_t = wire(GS.at[1 - c], GR, twin)

    sums = [jnp.concatenate(finish(run), axis=0) for run in (run_a, run_b)]
    text_pull = jnp.concatenate(sums, axis=0)
    text = te[...].astype(F32)
    text_norm = jnp.sqrt(jnp.sum(text * text, axis=1, keepdims=True) + EPS)
    text_unit = text / text_norm
    text_radial = jnp.sum(text_unit * text_pull, axis=1, keepdims=True)
    tg[...] = (text_pull - text_unit * text_radial) / text_norm

    o_t.wait_recv()
    for half in range(2):
        rows = pl.ds(half * 32, 32)
        GY[half, c] = GS[c, 1 - hi, rows].astype(BF16)
        GY[half, 1 - c] = GR[1 - hi, rows].astype(BF16)
    o_u = wire(GY.at[0], HU, up)
    o_d = wire(GY.at[1], HD, down)
    cg[hi, c] = GS[c, hi]
    cg[hi, 1 - c] = GR[hi]
    o_u.wait_recv()
    o_uu = wire(HU, HF.at[0], up)
    o_d.wait_recv()
    o_dd = wire(HD, HF.at[1], down)
    o_uu.wait_recv()
    o_dd.wait_recv()
    for k in range(2):
        cg[1 - hi, k, 0:32] = HF[0, k].astype(F32)
        cg[1 - hi, k, 32:64] = HF[1, k].astype(F32)
    wire.drain()


def shards(cell_states, projection, text_embeds, group_ids):
    vmem = pltpu.VMEM
    scratch = [
        vmem((8, 4, 32, WIDE), BF16),
        vmem((4, 4, 8, 128), I32),
        vmem((8, 2, 64, WIDE), BF16),
        vmem((8, 8, 128), I32),
        vmem((64, WIDE), F32),
        vmem((64, 128), F32),
        vmem((2, 64, WIDE), F32),
        vmem((2, 64, WIDE), F32),
        vmem((2, 64, WIDE), F32),
        vmem((32, WIDE), F32),
        vmem((32, WIDE), F32),
        vmem((64, WIDE), F32),
        vmem((64, WIDE), F32),
        vmem((8, 1, 128), F32),
        vmem((WIDE, 128), F32),
        vmem((4, WIDE, 256), BF16),
        vmem((8, 2, 2, 32, WIDE), F32),
        vmem((8, 2, 32, WIDE), BF16),
        vmem((8, 2, 32, WIDE), BF16),
        vmem((8, 2, 32, WIDE), BF16),
        vmem((2, 4, 2, 32, WIDE), BF16),
        vmem((8, 2, 64, WIDE), F32),
        vmem((8, 2, 64, WIDE), BF16),
        vmem((2, 2, 3, 64, WIDE), BF16),
        vmem((8, 2, 16, WIDE), F32),
        vmem((8, 2, 16, WIDE), BF16),
        vmem((2, 2, 3, 16, WIDE), BF16),
        vmem((2, 2, 64, 256), F32),
        vmem((2, 64, 256), F32),
        vmem((2, 2, 32, 256), BF16),
        vmem((2, 32, 256), BF16),
        vmem((2, 32, 256), BF16),
        vmem((2, 2, 32, 256), BF16),
        pltpu.SemaphoreType.DMA((COPIES,)),
        pltpu.SemaphoreType.DMA((COPIES,)),
    ]
    whole = pl.BlockSpec(memory_space=pltpu.VMEM)
    cell_grad, text_grad = pl.pallas_call(
        kernel,
        out_shape=(
            jax.ShapeDtypeStruct((2, 2, 64, 256), F32),
            jax.ShapeDtypeStruct((64, WIDE), F32),
        ),
        in_specs=[whole] * 4,
        out_specs=(whole, whole),
        scratch_shapes=scratch,
        compiler_params=pltpu.CompilerParams(
            collective_id=0, has_side_effects=True, vmem_limit_bytes=60 * 1024 * 1024
        ),
    )(
        cell_states.reshape(2, 2, 64, WIDE),
        projection,
        text_embeds,
        group_ids.reshape(2, 128),
    )
    return cell_grad.reshape(256, 256), text_grad


def solution(mesh):
    return jax.shard_map(
        shards,
        mesh=mesh,
        in_specs=(P("dp", "mp"), P("mp", None), P(("dp", "mp"), None), P("dp")),
        out_specs=(P("dp", "mp"), P(("dp", "mp"), None)),
        check_vma=False,
    )
```

```python
import jax
import jax.numpy as jnp
from jax import lax
from jax.experimental import pallas as pl
from jax.experimental.pallas import tpu as pltpu
from jax.sharding import PartitionSpec as P

MESH = pl.DeviceIdType.MESH
F32, BF16, I32 = jnp.float32, jnp.bfloat16, jnp.int32
WIDE = 1024
EPS = 1e-06
COPIES = 136
SLOT = {-3: 0, 3: 1, 4: 2, -4: 2, -2: 3, 2: 4, -1: 5, 1: 6, 0: 7}


class Wire:
    def __init__(self, send, recv):
        self.send, self.recv, self.open = send, recv, []

    def __call__(self, src, dst, where):
        i = len(self.open)
        copy = pltpu.make_async_remote_copy(
            src_ref=src,
            dst_ref=dst,
            send_sem=self.send.at[i],
            recv_sem=self.recv.at[i],
            device_id=where,
            device_id_type=MESH,
        )
        copy.start()
        self.open.append(copy)
        return copy

    def drain(self):
        for copy in self.open:
            copy.wait_send()


def dot(a, b, dims):
    return lax.dot_general(a, b, (dims, ((), ())), preferred_element_type=F32)


def kernel(
    cs, pj, te, ids, cg, tg,
    T, TI, CC, CI, CU, CN, TU, TN, PS, PO, PR, QS, FN,
    IDR, IDC, SL, CP, XS, XR, ZW, ZR,
    TP, W1, R1, W2, R2, GS, GR, GY, HF,
    send, recv,
):
    dp, mp = lax.axis_index("dp"), lax.axis_index("mp")
    x, z, ylo = dp // 16, lax.rem(dp // 2, 8), lax.rem(dp, 2)
    hi, c = mp // 2, lax.rem(mp, 2)
    y = hi * 2 + ylo

    def dev(x, y, z, c):
        return ((x * 8 + z) * 2 + lax.rem(y, 2), (y // 2) * 2 + c)

    xs = [dev(lax.rem(x + k, 4), y, z, c) for k in range(4)]
    ys = [dev(x, lax.rem(y + k, 4), z, c) for k in range(4)]
    zs = [dev(x, y, lax.rem(z + k, 8), c) for k in range(8)]
    front, back = zs[1], zs[7]
    twin, cross = dev(x, y, z, 1 - c), dev(x, lax.rem(y + 2, 4), z, 1 - c)

    barrier = pltpu.get_barrier_semaphore()
    peers = (*xs[1:], *ys[1:], *zs[1:], twin, cross)
    for where in peers:
        pl.semaphore_signal(barrier, inc=1, device_id=where, device_id_type=MESH)
    wire = Wire(send, recv)

    row = jnp.where(hi == 0, ids[0:1, :], ids[1:2, :])
    row = jnp.where(c == 0, row, jnp.roll(row, 64, axis=1))
    TI[0, 0] = jnp.broadcast_to(row, (8, 128))
    CI[0] = jnp.broadcast_to(row, (8, 128))

    text = te[...].astype(F32)
    text_norm = jnp.sqrt(jnp.sum(text * text, axis=1, keepdims=True) + EPS)
    text_unit = text / text_norm
    TU[...] = text_unit
    TN[...] = jnp.broadcast_to(text_norm, (64, 128))
    half = text_unit.astype(BF16)
    T[0, 0] = half[0:32]
    T[4, 0] = half[32:64]

    def project(core, out):
        rows = cs[:, core].reshape(128, WIDE)
        for n in range(4):
            cols = pl.ds(n * 256, 256)
            out[:, :, cols] = dot(rows, pj[:, cols], ((1,), (0,))).reshape(2, 64, 256)

    project(1 - c, PS)
    pl.semaphore_wait(barrier, len(peers))
    p_x = wire(PS, PR, twin)

    a1, b1, ix = [], [], []
    for k in (2, 1, 3):
        a1.append(wire(T.at[0, 0], T.at[0, 4 - k], xs[k]))
        b1.append(wire(T.at[4, 0], T.at[4, 4 - k], ys[k]))
        ix.append(wire(TI.at[0, 0], TI.at[0, 4 - k], xs[k]))
    iz = [wire(CI.at[0], CI.at[8 - k], zs[k]) for k in range(1, 8)]

    project(c, PO)
    p_x.wait_recv()
    QS[...] = (PO[1 - hi] + PR[1 - hi]).astype(BF16)
    q = wire(QS, FN, ys[2])
    PO[0] = PO[hi] + PR[hi]

    for copy in a1:
        copy.wait_recv()
    a2 = [wire(T.at[0], T.at[4 - k], ys[k]) for k in (2, 1, 3)]
    for copy in b1:
        copy.wait_recv()
    b2 = [wire(T.at[4], T.at[8 - k], xs[k]) for k in (2, 1, 3)]
    for copy in ix:
        copy.wait_recv()
    iy = [wire(TI.at[0], TI.at[4 - k], ys[k]) for k in (2, 1, 3)]

    q.wait_recv()
    emb = PO[0] + FN[...].astype(F32)
    cell_norm = jnp.sqrt(jnp.sum(emb * emb, axis=1, keepdims=True) + EPS)
    unit = emb / cell_norm
    CU[...] = unit
    CN[...] = jnp.broadcast_to(cell_norm, (64, 128))
    CC[7, 0] = unit.astype(BF16)

    def piece(p):
        return pl.ds(16 * p, 16)

    def pass_on(k, p, step, where):
        return wire(
            CC.at[SLOT[k], 0, piece(p)], CC.at[SLOT[k + step], 0, piece(p)], where
        )

    g_f = {p: pass_on(0, p, -1, front) for p in range(4)}
    g_b = {p: pass_on(0, p, 1, back) for p in (3, 2, 1, 0)}
    g_t = {7: wire(CC.at[7, 0], CC.at[7, 1], twin)}
    for k in range(1, 4):
        n_f, n_b = {}, {}
        for p in range(4):
            g_f[p].wait_recv()
            if k < 3 or p < 2:
                n_f[p] = pass_on(-k, p, -1, front)
            g_b[3 - p].wait_recv()
            if k < 3 or p < 2:
                n_b[3 - p] = pass_on(k, 3 - p, 1, back)
        g_f, g_b = n_f, n_b
        for s in (SLOT[-k], SLOT[k]):
            g_t[s] = wire(CC.at[s, 0], CC.at[s, 1], twin)

    for copy in (*iy, *iz):
        copy.wait_recv()
    lane = lax.broadcasted_iota(I32, (1, 128), 1)
    for h in range(2):
        for a in range(4):
            parts = [TI[a, b, 0:1] if h == 0 else TI[b, a, 0:1] for b in range(4)]
            names = jnp.zeros((1, 128), I32)
            for b in range(4):
                moved = parts[b]
                if (b - h) % 4:
                    moved = jnp.roll(moved, 32 * ((b - h) % 4), axis=1)
                names = jnp.where(lane // 32 == b, moved, names)
            IDR[h * 4 + a] = names.astype(F32)
    for k, s in SLOT.items():
        if k != -4:
            IDC[s] = jnp.broadcast_to(CI[k % 8, 0:1, :].astype(F32), (128, 128)).T
    for copy in (*a2, *b2):
        copy.wait_recv()

    def chunk(s, n):
        rows = n * 128
        cells = CC[s : s + n].reshape(rows, WIDE)
        col = IDC[s : s + n].reshape(rows, 128)
        col = jnp.concatenate([col, col], axis=1)
        for t in range(4):
            inner = dot(cells, T[2 * t : 2 * t + 2].reshape(256, WIDE), ((1,), (1,)))
            names = jnp.concatenate([IDR[t * 2], IDR[t * 2 + 1]], axis=1)
            slope = 5.0 * jnp.tanh(5.0 * inner - 2.0) + jnp.where(col == names, -5.0, 5.0)
            SL[t, s * 128 : s * 128 + rows, :] = slope.astype(BF16)
        slopes = [SL[t, s * 128 : s * 128 + rows, :] for t in range(4)]
        total = dot(jnp.concatenate(slopes, axis=1), T[...].reshape(WIDE, WIDE), ((1,), (0,)))
        total = total.reshape(n, 2, 4, 16, WIDE)
        CP[s : s + n] = total[:, 0]
        XS[s : s + n] = total[:, 1].astype(BF16)
        return wire(XS.at[pl.ds(s, n)], XR.at[pl.ds(s, n)], twin)

    def zput(k, p, add=None):
        s = SLOT[k]
        v = CP[s, p] + XR[s, p].astype(F32)
        if add is not None:
            v = v + ZR[add[0], add[1], p].astype(F32)
        ZW[s, p] = v.astype(BF16)
        return ZW.at[s, p]

    def zsend(way, hop, p, add=True):
        k = (4 - hop) * (1, -1)[way]
        return wire(
            zput(k, p, (way, hop - 1) if add else None),
            ZR.at[way, hop, p],
            (front, back)[way],
        )

    for s in (0, 1):
        g_t[s].wait_recv()
    x_3 = chunk(0, 2)
    for copy in (*g_f.values(), *g_b.values()):
        copy.wait_recv()
    g_t[2] = wire(CC.at[2, 0], CC.at[2, 1], twin)
    g_t[2].wait_recv()
    x_4 = chunk(2, 1)
    for s in (3, 4):
        g_t[s].wait_recv()
    x_2 = chunk(3, 2)
    x_4.wait_recv()
    z0 = [{p: zsend(0, 0, p, False) for p in (0, 1)}, {p: zsend(1, 0, p, False) for p in (3, 2)}]
    x_3.wait_recv()
    z1 = [{p: zsend(0, 1, p, False) for p in (2, 3)}, {p: zsend(1, 1, p, False) for p in (1, 0)}]
    for s in (5, 6):
        g_t[s].wait_recv()
    x_1 = chunk(5, 2)
    g_t[7].wait_recv()
    x_0 = chunk(7, 1)

    def zhop(hop, prev, new, pieces):
        for i in range(len(pieces)):
            for way in range(2):
                p = pieces[i] if way == 0 else 3 - pieces[i]
                prev[way][p].wait_recv()
                new[way][p] = zsend(way, hop, p)

    cells_all = CC[...].reshape(WIDE, WIDE)

    def text_tiles(h):
        for t in (2 * h, 2 * h + 1):
            total = dot(SL[t], cells_all, ((0,), (0,)))
            total = total.reshape(2, 4, 32, WIDE)
            TP[2 * t : 2 * t + 2] = total
            W1[2 * t : 2 * t + 2] = total.astype(BF16)

    def text_send(h):
        to = (ys, xs)[h]
        return {
            (j2, j1): wire(W1.at[4 * h + j1, j2], R1.at[h, j1 - 1, j2], to[j1])
            for j2 in (2, 1, 3, 0)
            for j1 in (2, 1, 3)
        }

    text_tiles(0)
    t1 = [text_send(0)]
    zhop(1, z0, z1, (0, 1))
    text_tiles(1)
    t1.append(text_send(1))

    def text_sum(h, j2):
        for j1 in (2, 1, 3):
            t1[h][j2, j1].wait_recv()
        return TP[4 * h, j2] + sum(R1[h, j, j2].astype(F32) for j in range(3))

    t2 = [{}, {}]

    def text_round(j2):
        for h in range(2):
            W2[h, j2] = text_sum(h, j2).astype(BF16)
            t2[h][j2] = wire(W2.at[h, j2], R2.at[h, j2 - 1], (xs, ys)[h][j2])

    x_2.wait_recv()
    z2 = [{}, {}]
    zhop(2, z1, z2, (2, 3, 0, 1))
    text_round(2)
    x_1.wait_recv()
    z3 = [{}, {}]
    zhop(3, z2, z3, (2, 3, 0, 1))
    text_round(1)

    x_0.wait_recv()
    for way in range(2):
        for copy in z3[way].values():
            copy.wait_recv()
    pull = CP[7] + XR[7].astype(F32) + ZR[0, 3].astype(F32) + ZR[1, 3].astype(F32)
    pull = pull.reshape(64, WIDE)
    unit = CU[...]
    radial = jnp.sum(unit * pull, axis=1, keepdims=True)
    grad = (pull - unit * radial) / CN[:, 0:1]
    for h in range(2):
        for k in range(2):
            cols = grad[:, (h * 2 + k) * 256 : (h * 2 + k + 1) * 256]
            GS[h, k] = cols
            GY[h, k] = cols.astype(BF16)
    o_y = wire(GY.at[1 - hi, c], HF.at[0], ys[2])
    o_m = wire(GY.at[1 - hi, 1 - c], HF.at[1], cross)
    o_t = wire(GS.at[hi, 1 - c], GR, twin)
    cg[hi, c] = GS[hi, c]

    text_round(3)
    text_pull = [text_sum(h, 0) for h in range(2)]
    for h in range(2):
        for copy in t2[h].values():
            copy.wait_recv()
        text_pull[h] = text_pull[h] + sum(R2[h, j].astype(F32) for j in range(3))
    text_pull = jnp.concatenate(text_pull, axis=0)
    text_unit = TU[...]
    text_radial = jnp.sum(text_unit * text_pull, axis=1, keepdims=True)
    tg[...] = (text_pull - text_unit * text_radial) / TN[:, 0:1]

    for copy in (o_t, o_y, o_m):
        copy.wait_recv()
    cg[hi, 1 - c] = GR[...]
    cg[1 - hi, c] = HF[0].astype(F32)
    cg[1 - hi, 1 - c] = HF[1].astype(F32)
    wire.drain()


def shards(cell_states, projection, text_embeds, group_ids):
    vmem = pltpu.VMEM
    scratch = [
        vmem((8, 4, 32, WIDE), BF16),
        vmem((4, 4, 8, 128), I32),
        vmem((8, 2, 64, WIDE), BF16),
        vmem((8, 8, 128), I32),
        vmem((64, WIDE), F32),
        vmem((64, 128), F32),
        vmem((64, WIDE), F32),
        vmem((64, 128), F32),
        vmem((2, 64, WIDE), F32),
        vmem((2, 64, WIDE), F32),
        vmem((2, 64, WIDE), F32),
        vmem((64, WIDE), BF16),
        vmem((64, WIDE), BF16),
        vmem((8, 1, 128), F32),
        vmem((8, 128, 128), F32),
        vmem((4, WIDE, 256), BF16),
        vmem((8, 4, 16, WIDE), F32),
        vmem((8, 4, 16, WIDE), BF16),
        vmem((8, 4, 16, WIDE), BF16),
        vmem((8, 4, 16, WIDE), BF16),
        vmem((2, 4, 4, 16, WIDE), BF16),
        vmem((8, 4, 32, WIDE), F32),
        vmem((8, 4, 32, WIDE), BF16),
        vmem((2, 3, 4, 32, WIDE), BF16),
        vmem((2, 4, 32, WIDE), BF16),
        vmem((2, 3, 32, WIDE), BF16),
        vmem((2, 2, 64, 256), F32),
        vmem((64, 256), F32),
        vmem((2, 2, 64, 256), BF16),
        vmem((2, 64, 256), BF16),
        pltpu.SemaphoreType.DMA((COPIES,)),
        pltpu.SemaphoreType.DMA((COPIES,)),
    ]
    whole = pl.BlockSpec(memory_space=pltpu.VMEM)
    cell_grad, text_grad = pl.pallas_call(
        kernel,
        out_shape=(
            jax.ShapeDtypeStruct((2, 2, 64, 256), F32),
            jax.ShapeDtypeStruct((64, WIDE), F32),
        ),
        in_specs=[whole] * 4,
        out_specs=(whole, whole),
        scratch_shapes=scratch,
        compiler_params=pltpu.CompilerParams(
            collective_id=0, has_side_effects=True, vmem_limit_bytes=60 * 1024 * 1024
        ),
    )(
        cell_states.reshape(2, 2, 64, WIDE),
        projection,
        text_embeds,
        group_ids.reshape(2, 128),
    )
    return cell_grad.reshape(256, 256), text_grad


def solution(mesh):
    return jax.shard_map(
        shards,
        mesh=mesh,
        in_specs=(P("dp", "mp"), P("mp", None), P(("dp", "mp"), None), P("dp")),
        out_specs=(P("dp", "mp"), P(("dp", "mp"), None)),
        check_vma=False,
    )
```

```python
import jax
import jax.numpy as jnp
from jax import lax
from jax.experimental import pallas as pl
from jax.experimental.pallas import tpu as pltpu
from jax.sharding import PartitionSpec as P

MESH = pl.DeviceIdType.MESH
F32, BF16, I32 = jnp.float32, jnp.bfloat16, jnp.int32
WIDE = 1024
EPS = 1e-06
COPIES = 136
SLOT = {-3: 0, 3: 1, 4: 2, -4: 2, -2: 3, 2: 4, -1: 5, 1: 6, 0: 7}


class Wire:
    def __init__(self, send, recv):
        self.send, self.recv, self.open = send, recv, []

    def __call__(self, src, dst, where):
        i = len(self.open)
        copy = pltpu.make_async_remote_copy(
            src_ref=src,
            dst_ref=dst,
            send_sem=self.send.at[i],
            recv_sem=self.recv.at[i],
            device_id=where,
            device_id_type=MESH,
        )
        copy.start()
        self.open.append(copy)
        return copy

    def drain(self):
        for copy in self.open:
            copy.wait_send()


def dot(a, b, dims):
    return lax.dot_general(a, b, (dims, ((), ())), preferred_element_type=F32)


def kernel(
    cs, pj, te, ids, cg, tg,
    T, TI, CC, CI, CU, CN, TU, TN, PO, PR, QS, FN,
    IDR, IDC, SL, CP, XS, XR, ZW, ZR,
    TP, W1, R1, W2, R2, GS, GR, GY, HF,
    send, recv,
):
    dp, mp = lax.axis_index("dp"), lax.axis_index("mp")
    x, z, ylo = dp // 16, lax.rem(dp // 2, 8), lax.rem(dp, 2)
    hi, c = mp // 2, lax.rem(mp, 2)
    y = hi * 2 + ylo

    def dev(x, y, z, c):
        return ((x * 8 + z) * 2 + lax.rem(y, 2), (y // 2) * 2 + c)

    xs = [dev(lax.rem(x + k, 4), y, z, c) for k in range(4)]
    ys = [dev(x, lax.rem(y + k, 4), z, c) for k in range(4)]
    zs = [dev(x, y, lax.rem(z + k, 8), c) for k in range(8)]
    front, back = zs[1], zs[7]
    twin, cross = dev(x, y, z, 1 - c), dev(x, lax.rem(y + 2, 4), z, 1 - c)

    barrier = pltpu.get_barrier_semaphore()
    peers = (*xs[1:], *ys[1:], *zs[1:], twin, cross)
    for where in peers:
        pl.semaphore_signal(barrier, inc=1, device_id=where, device_id_type=MESH)
    wire = Wire(send, recv)

    row = jnp.where(hi == 0, ids[0:1, :], ids[1:2, :])
    row = jnp.where(c == 0, row, jnp.roll(row, 64, axis=1))
    TI[0, 0] = jnp.broadcast_to(row, (8, 128))
    CI[0] = jnp.broadcast_to(row, (8, 128))

    text = te[...].astype(F32)
    text_norm = jnp.sqrt(jnp.sum(text * text, axis=1, keepdims=True) + EPS)
    text_unit = text / text_norm
    TU[...] = text_unit
    TN[...] = jnp.broadcast_to(text_norm, (64, 128))
    half = text_unit.astype(BF16)
    T[0, 0] = half[0:32]
    T[4, 0] = half[32:64]

    rows = cs[...].reshape(256, WIDE)
    for n in range(4):
        cols = pl.ds(n * 256, 256)
        part = dot(rows, pj[:, cols], ((1,), (0,))).reshape(2, 2, 64, 256)
        PO[0, :, :, cols] = part[:, 0]
        PO[1, :, :, cols] = part[:, 1]
    pl.semaphore_wait(barrier, len(peers))
    p_x = wire(PO.at[1 - c], PR, twin)

    a1 = [wire(T.at[0, 0], T.at[0, 4 - k], xs[k]) for k in (2, 1, 3)]
    b1 = [wire(T.at[4, 0], T.at[4, 4 - k], ys[k]) for k in (1, 3)]
    ix = [wire(TI.at[0, 0], TI.at[0, 4 - k], xs[k]) for k in range(1, 4)]
    iz = [wire(CI.at[0], CI.at[8 - k], zs[k]) for k in range(1, 8)]

    p_x.wait_recv()
    QS[...] = (PO[c, 1 - hi] + PR[1 - hi]).astype(BF16)
    q = wire(QS, FN, ys[2])
    b1.append(wire(T.at[4, 0], T.at[4, 2], ys[2]))
    PR[0] = PO[c, hi] + PR[hi]

    for copy in a1:
        copy.wait_recv()
    a2 = [wire(T.at[0], T.at[4 - k], ys[k]) for k in (2, 1, 3)]
    for copy in ix:
        copy.wait_recv()
    iy = [wire(TI.at[0], TI.at[4 - k], ys[k]) for k in (2, 1, 3)]
    for copy in b1:
        copy.wait_recv()
    b2 = [wire(T.at[4], T.at[8 - k], xs[k]) for k in (2, 1, 3)]

    q.wait_recv()
    emb = PR[0] + FN[...].astype(F32)
    cell_norm = jnp.sqrt(jnp.sum(emb * emb, axis=1, keepdims=True) + EPS)
    unit = emb / cell_norm
    CU[...] = unit
    CN[...] = jnp.broadcast_to(cell_norm, (64, 128))
    CC[7, 0] = unit.astype(BF16)

    def piece(p):
        return pl.ds(16 * p, 16)

    def pass_on(k, p, step, where):
        return wire(
            CC.at[SLOT[k], 0, piece(p)], CC.at[SLOT[k + step], 0, piece(p)], where
        )

    g_f = {p: pass_on(0, p, -1, front) for p in range(4)}
    g_b = {p: pass_on(0, p, 1, back) for p in (3, 2, 1, 0)}
    g_t = {7: wire(CC.at[7, 0], CC.at[7, 1], twin)}
    for k in range(1, 4):
        n_f, n_b = {}, {}
        for p in range(4):
            g_f[p].wait_recv()
            if k < 3 or p < 2:
                n_f[p] = pass_on(-k, p, -1, front)
            g_b[3 - p].wait_recv()
            if k < 3 or p < 2:
                n_b[3 - p] = pass_on(k, 3 - p, 1, back)
        g_f, g_b = n_f, n_b
        for s in (SLOT[-k], SLOT[k]):
            g_t[s] = wire(CC.at[s, 0], CC.at[s, 1], twin)

    for copy in (*iy, *iz):
        copy.wait_recv()
    lane = lax.broadcasted_iota(I32, (1, 128), 1)
    for h in range(2):
        for a in range(4):
            parts = [TI[a, b, 0:1] if h == 0 else TI[b, a, 0:1] for b in range(4)]
            names = jnp.zeros((1, 128), I32)
            for b in range(4):
                moved = parts[b]
                if (b - h) % 4:
                    moved = jnp.roll(moved, 32 * ((b - h) % 4), axis=1)
                names = jnp.where(lane // 32 == b, moved, names)
            IDR[h * 4 + a] = names.astype(F32)
    for k, s in SLOT.items():
        if k != -4:
            IDC[s] = jnp.broadcast_to(CI[k % 8, 0:1, :].astype(F32), (128, 128)).T
    for copy in (*a2, *b2):
        copy.wait_recv()

    def slopes(s, n):
        rows = n * 128
        cells = CC[s : s + n].reshape(rows, WIDE)
        col = IDC[s : s + n].reshape(rows, 128)
        col = jnp.concatenate([col, col], axis=1)
        for t in range(4):
            inner = dot(cells, T[2 * t : 2 * t + 2].reshape(256, WIDE), ((1,), (1,)))
            names = jnp.concatenate([IDR[t * 2], IDR[t * 2 + 1]], axis=1)
            slope = 5.0 * jnp.tanh(5.0 * inner - 2.0) + jnp.where(col == names, -5.0, 5.0)
            SL[t, s * 128 : s * 128 + rows, :] = slope.astype(BF16)

    def pulls(s, n):
        rows = n * 128
        left = [SL[t, s * 128 : s * 128 + rows, :] for t in range(4)]
        total = dot(jnp.concatenate(left, axis=1), T[...].reshape(WIDE, WIDE), ((1,), (0,)))
        total = total.reshape(n, 2, 4, 16, WIDE)
        CP[s : s + n] = total[:, 0]
        XS[s : s + n] = total[:, 1].astype(BF16)

    def swap(s, n):
        return wire(XS.at[pl.ds(s, n)], XR.at[pl.ds(s, n)], twin)

    def zput(k, p, add=None):
        s = SLOT[k]
        v = CP[s, p] + XR[s, p].astype(F32)
        if add is not None:
            v = v + ZR[add[0], add[1], p].astype(F32)
        ZW[s, p] = v.astype(BF16)
        return ZW.at[s, p]

    def zsend(way, hop, p, add=True):
        k = (4 - hop) * (1, -1)[way]
        return wire(
            zput(k, p, (way, hop - 1) if add else None),
            ZR.at[way, hop, p],
            (front, back)[way],
        )

    def zhop(hop, prev, new, pieces):
        for i in range(len(pieces)):
            for way in range(2):
                p = pieces[i] if way == 0 else 3 - pieces[i]
                prev[way][p].wait_recv()
                new[way][p] = zsend(way, hop, p)

    def text_tile(h):
        left = jnp.concatenate([SL[2 * h], SL[2 * h + 1]], axis=1)
        total = dot(left, CC[...].reshape(WIDE, WIDE), ((0,), (0,)))
        total = total.reshape(4, 4, 32, WIDE)
        TP[4 * h : 4 * h + 4] = total
        W1[4 * h : 4 * h + 4] = total.astype(BF16)

    def text_send(h):
        to = (ys, xs)[h]
        return {
            (j2, j1): wire(W1.at[4 * h + j1, j2], R1.at[h, j1 - 1, j2], to[j1])
            for j2 in (2, 1, 3, 0)
            for j1 in (2, 1, 3)
        }

    for s in range(3, 8):
        g_t[s].wait_recv()
    slopes(3, 5)
    for copy in (*g_f.values(), *g_b.values()):
        copy.wait_recv()
    g_t[2] = wire(CC.at[2, 0], CC.at[2, 1], twin)
    for s in (0, 1, 2):
        g_t[s].wait_recv()
    slopes(0, 3)
    pulls(0, 3)
    x_4, x_3 = swap(2, 1), swap(0, 2)
    text_tile(0)
    t1 = [text_send(0)]
    x_4.wait_recv()
    z0 = [{p: zsend(0, 0, p, False) for p in (0, 1)}, {p: zsend(1, 0, p, False) for p in (3, 2)}]
    x_3.wait_recv()
    z1 = [{p: zsend(0, 1, p, False) for p in (2, 3)}, {p: zsend(1, 1, p, False) for p in (1, 0)}]
    text_tile(1)
    t1.append(text_send(1))
    pulls(3, 5)
    x_2, x_1, x_0 = swap(3, 2), swap(5, 2), swap(7, 1)
    zhop(1, z0, z1, (0, 1))

    def text_sum(h, j2):
        for j1 in (2, 1, 3):
            t1[h][j2, j1].wait_recv()
        return TP[4 * h, j2] + sum(R1[h, j, j2].astype(F32) for j in range(3))

    t2 = [{}, {}]

    def text_round(j2):
        for h in range(2):
            W2[h, j2] = text_sum(h, j2).astype(BF16)
            t2[h][j2] = wire(W2.at[h, j2], R2.at[h, j2 - 1], (xs, ys)[h][j2])

    x_2.wait_recv()
    z2 = [{}, {}]
    zhop(2, z1, z2, (2, 3, 0, 1))
    text_round(2)
    x_1.wait_recv()
    z3 = [{}, {}]
    zhop(3, z2, z3, (2, 3, 0, 1))
    text_round(1)

    x_0.wait_recv()
    for way in range(2):
        for copy in z3[way].values():
            copy.wait_recv()
    pull = CP[7] + XR[7].astype(F32) + ZR[0, 3].astype(F32) + ZR[1, 3].astype(F32)
    pull = pull.reshape(64, WIDE)
    unit = CU[...]
    radial = jnp.sum(unit * pull, axis=1, keepdims=True)
    grad = (pull - unit * radial) / CN[:, 0:1]
    for h in range(2):
        for k in range(2):
            cols = grad[:, (h * 2 + k) * 256 : (h * 2 + k + 1) * 256]
            GS[h, k] = cols
            GY[h, k] = cols.astype(BF16)
    o_y = wire(GY.at[1 - hi, c], HF.at[0], ys[2])
    o_m = wire(GY.at[1 - hi, 1 - c], HF.at[1], cross)
    o_t = wire(GS.at[hi, 1 - c], GR, twin)
    cg[hi, c] = GS[hi, c]

    text_round(3)
    text_pull = [text_sum(h, 0) for h in range(2)]
    for h in range(2):
        for copy in t2[h].values():
            copy.wait_recv()
        text_pull[h] = text_pull[h] + sum(R2[h, j].astype(F32) for j in range(3))
    text_pull = jnp.concatenate(text_pull, axis=0)
    text_unit = TU[...]
    text_radial = jnp.sum(text_unit * text_pull, axis=1, keepdims=True)
    tg[...] = (text_pull - text_unit * text_radial) / TN[:, 0:1]

    for copy in (o_t, o_y, o_m):
        copy.wait_recv()
    cg[hi, 1 - c] = GR[...]
    cg[1 - hi, c] = HF[0].astype(F32)
    cg[1 - hi, 1 - c] = HF[1].astype(F32)
    wire.drain()


def shards(cell_states, projection, text_embeds, group_ids):
    vmem = pltpu.VMEM
    scratch = [
        vmem((8, 4, 32, WIDE), BF16),
        vmem((4, 4, 8, 128), I32),
        vmem((8, 2, 64, WIDE), BF16),
        vmem((8, 8, 128), I32),
        vmem((64, WIDE), F32),
        vmem((64, 128), F32),
        vmem((64, WIDE), F32),
        vmem((64, 128), F32),
        vmem((2, 2, 64, WIDE), F32),
        vmem((2, 64, WIDE), F32),
        vmem((64, WIDE), BF16),
        vmem((64, WIDE), BF16),
        vmem((8, 1, 128), F32),
        vmem((8, 128, 128), F32),
        vmem((4, WIDE, 256), BF16),
        vmem((8, 4, 16, WIDE), F32),
        vmem((8, 4, 16, WIDE), BF16),
        vmem((8, 4, 16, WIDE), BF16),
        vmem((8, 4, 16, WIDE), BF16),
        vmem((2, 4, 4, 16, WIDE), BF16),
        vmem((8, 4, 32, WIDE), F32),
        vmem((8, 4, 32, WIDE), BF16),
        vmem((2, 3, 4, 32, WIDE), BF16),
        vmem((2, 4, 32, WIDE), BF16),
        vmem((2, 3, 32, WIDE), BF16),
        vmem((2, 2, 64, 256), F32),
        vmem((64, 256), F32),
        vmem((2, 2, 64, 256), BF16),
        vmem((2, 64, 256), BF16),
        pltpu.SemaphoreType.DMA((COPIES,)),
        pltpu.SemaphoreType.DMA((COPIES,)),
    ]
    whole = pl.BlockSpec(memory_space=pltpu.VMEM)
    cell_grad, text_grad = pl.pallas_call(
        kernel,
        out_shape=(
            jax.ShapeDtypeStruct((2, 2, 64, 256), F32),
            jax.ShapeDtypeStruct((64, WIDE), F32),
        ),
        in_specs=[whole] * 4,
        out_specs=(whole, whole),
        scratch_shapes=scratch,
        compiler_params=pltpu.CompilerParams(
            collective_id=0, has_side_effects=True, vmem_limit_bytes=34 * 1024 * 1024
        ),
    )(
        cell_states.reshape(2, 2, 64, WIDE),
        projection,
        text_embeds,
        group_ids.reshape(2, 128),
    )
    return cell_grad.reshape(256, 256), text_grad


def solution(mesh):
    return jax.shard_map(
        shards,
        mesh=mesh,
        in_specs=(P("dp", "mp"), P("mp", None), P(("dp", "mp"), None), P("dp")),
        out_specs=(P("dp", "mp"), P(("dp", "mp"), None)),
        check_vma=False,
    )
```

```python
import jax
import jax.numpy as jnp
from jax import lax
from jax.experimental import pallas as pl
from jax.experimental.pallas import tpu as pltpu
from jax.sharding import PartitionSpec as P

MESH = pl.DeviceIdType.MESH
F32, BF16, I32 = jnp.float32, jnp.bfloat16, jnp.int32
WIDE = 1024
EPS = 1e-06
COPIES = 160
SLOT = {-3: 0, 3: 1, 4: 2, -4: 2, -2: 3, 2: 4, -1: 5, 1: 6, 0: 7}


class Wire:
    def __init__(self, send, recv):
        self.send, self.recv, self.open = send, recv, []

    def __call__(self, src, dst, where):
        i = len(self.open)
        copy = pltpu.make_async_remote_copy(
            src_ref=src,
            dst_ref=dst,
            send_sem=self.send.at[i],
            recv_sem=self.recv.at[i],
            device_id=where,
            device_id_type=MESH,
        )
        copy.start()
        self.open.append(copy)
        return copy

    def drain(self):
        for copy in self.open:
            copy.wait_send()


def dot(a, b, dims):
    return lax.dot_general(a, b, (dims, ((), ())), preferred_element_type=F32)


def kernel(
    cs_hbm, pj_hbm, te_hbm, ids_hbm, cg, tg,
    cs, pj, te, ids, load,
    T, TI, CC, CI, CU, CN, TU, TN, PO, PR, QS, FN,
    IDR, IDC, SL, CP, XS, XR, ZW, ZR,
    TP, W1, R1, W2, R2, GS, GR, GY, HF,
    send, recv,
):
    dp, mp = lax.axis_index("dp"), lax.axis_index("mp")
    x, z, ylo = dp // 16, lax.rem(dp // 2, 8), lax.rem(dp, 2)
    hi, c = mp // 2, lax.rem(mp, 2)
    y = hi * 2 + ylo

    def dev(x, y, z, c):
        return ((x * 8 + z) * 2 + lax.rem(y, 2), (y // 2) * 2 + c)

    xs = [dev(lax.rem(x + k, 4), y, z, c) for k in range(4)]
    ys = [dev(x, lax.rem(y + k, 4), z, c) for k in range(4)]
    zs = [dev(x, y, lax.rem(z + k, 8), c) for k in range(8)]
    front, back = zs[1], zs[7]
    twin, cross = dev(x, y, z, 1 - c), dev(x, lax.rem(y + 2, 4), z, 1 - c)

    loads = [
        pltpu.make_async_copy(te_hbm, te, load.at[0]),
        pltpu.make_async_copy(ids_hbm, ids, load.at[1]),
        pltpu.make_async_copy(cs_hbm, cs, load.at[2]),
    ]
    for n in range(4):
        cols = pl.ds(n * 256, 256)
        loads.append(pltpu.make_async_copy(pj_hbm.at[:, cols], pj.at[n], load.at[3 + n]))
    for copy in loads:
        copy.start()

    barrier = pltpu.get_barrier_semaphore()
    peers = (*xs[1:], *ys[1:], *zs[1:], twin, cross)
    for where in peers:
        pl.semaphore_signal(barrier, inc=1, device_id=where, device_id_type=MESH)
    wire = Wire(send, recv)

    loads[1].wait()
    row = jnp.where(hi == 0, ids[0:1, :], ids[1:2, :])
    row = jnp.where(c == 0, row, jnp.roll(row, 64, axis=1))
    TI[0, 0] = jnp.broadcast_to(row, (8, 128))
    CI[0] = jnp.broadcast_to(row, (8, 128))

    loads[0].wait()
    text = te[...].astype(F32)
    text_norm = jnp.sqrt(jnp.sum(text * text, axis=1, keepdims=True) + EPS)
    text_unit = text / text_norm
    TU[...] = text_unit
    TN[...] = jnp.broadcast_to(text_norm, (64, 128))
    half = text_unit.astype(BF16)
    T[0, 0] = half[0:32]
    T[4, 0] = half[32:64]

    loads[2].wait()
    rows = cs[...].reshape(256, WIDE)
    for n in range(4):
        cols = pl.ds(n * 256, 256)
        loads[3 + n].wait()
        part = dot(rows, pj[n], ((1,), (0,))).reshape(2, 2, 64, 256)
        PO[0, :, :, cols] = part[:, 0]
        PO[1, :, :, cols] = part[:, 1]
    pl.semaphore_wait(barrier, len(peers))
    p_x = wire(PO.at[1 - c], PR, twin)

    def spread(h, block):
        to = (ys, xs)[h]
        return [
            wire(T.at[4 * h, block], T.at[4 * h + 4 - k, block], to[k]) for k in (1, 3, 2)
        ]

    a1 = {4 - k: wire(T.at[0, 0], T.at[0, 4 - k], xs[k]) for k in (1, 3)}
    b1 = {4 - k: wire(T.at[4, 0], T.at[4, 4 - k], ys[k]) for k in (1, 3)}
    a1[2] = wire(T.at[0, 0], T.at[0, 2], xs[2])
    ix = [wire(TI.at[0, 0], TI.at[0, 4 - k], xs[k]) for k in range(1, 4)]
    iz = [wire(CI.at[0], CI.at[8 - k], zs[k]) for k in range(1, 8)]
    b2 = spread(1, 0)

    p_x.wait_recv()
    QS[...] = (PO[c, 1 - hi] + PR[1 - hi]).astype(BF16)
    q = wire(QS, FN, ys[2])
    b1[2] = wire(T.at[4, 0], T.at[4, 2], ys[2])
    a2 = spread(0, 0)
    PR[0] = PO[c, hi] + PR[hi]

    for block in (3, 1):
        b1[block].wait_recv()
        b2 += spread(1, block)
    for block in (3, 1, 2):
        a1[block].wait_recv()
        a2 += spread(0, block)
    for copy in ix:
        copy.wait_recv()
    iy = [wire(TI.at[0], TI.at[4 - k], ys[k]) for k in (2, 1, 3)]

    q.wait_recv()
    emb = PR[0] + FN[...].astype(F32)
    cell_norm = jnp.sqrt(jnp.sum(emb * emb, axis=1, keepdims=True) + EPS)
    unit = emb / cell_norm
    CU[...] = unit
    CN[...] = jnp.broadcast_to(cell_norm, (64, 128))
    CC[7, 0] = unit.astype(BF16)

    def piece(p):
        return pl.ds(16 * p, 16)

    def pass_on(k, p, step, where):
        return wire(
            CC.at[SLOT[k], 0, piece(p)], CC.at[SLOT[k + step], 0, piece(p)], where
        )

    g_f = {p: pass_on(0, p, -1, front) for p in range(4)}
    g_b = {p: pass_on(0, p, 1, back) for p in (3, 2, 1, 0)}
    g_t = {7: wire(CC.at[7, 0], CC.at[7, 1], twin)}
    b1[2].wait_recv()
    b2 += spread(1, 2)
    for k in range(1, 4):
        n_f, n_b = {}, {}
        for p in range(4):
            g_f[p].wait_recv()
            if k < 3 or p < 2:
                n_f[p] = pass_on(-k, p, -1, front)
            g_b[3 - p].wait_recv()
            if k < 3 or p < 2:
                n_b[3 - p] = pass_on(k, 3 - p, 1, back)
        g_f, g_b = n_f, n_b
        for s in (SLOT[-k], SLOT[k]):
            g_t[s] = wire(CC.at[s, 0], CC.at[s, 1], twin)

    for copy in (*iy, *iz):
        copy.wait_recv()
    lane = lax.broadcasted_iota(I32, (1, 128), 1)
    for h in range(2):
        for a in range(4):
            parts = [TI[a, b, 0:1] if h == 0 else TI[b, a, 0:1] for b in range(4)]
            names = jnp.zeros((1, 128), I32)
            for b in range(4):
                moved = parts[b]
                if (b - h) % 4:
                    moved = jnp.roll(moved, 32 * ((b - h) % 4), axis=1)
                names = jnp.where(lane // 32 == b, moved, names)
            IDR[h * 4 + a] = names.astype(F32)
    for k, s in SLOT.items():
        if k != -4:
            IDC[s] = jnp.broadcast_to(CI[k % 8, 0:1, :].astype(F32), (128, 128)).T
    for copy in b2:
        copy.wait_recv()

    def slopes(s, n, tiles=(2, 3, 0, 1)):
        rows = n * 128
        cells = CC[s : s + n].reshape(rows, WIDE)
        col = IDC[s : s + n].reshape(rows, 128)
        col = jnp.concatenate([col, col], axis=1)
        for t in tiles:
            inner = dot(cells, T[2 * t : 2 * t + 2].reshape(256, WIDE), ((1,), (1,)))
            names = jnp.concatenate([IDR[t * 2], IDR[t * 2 + 1]], axis=1)
            slope = 5.0 * jnp.tanh(5.0 * inner - 2.0) + jnp.where(col == names, -5.0, 5.0)
            SL[t, s * 128 : s * 128 + rows, :] = slope.astype(BF16)

    def pulls(s, n):
        rows = n * 128
        left = [SL[t, s * 128 : s * 128 + rows, :] for t in range(4)]
        total = dot(jnp.concatenate(left, axis=1), T[...].reshape(WIDE, WIDE), ((1,), (0,)))
        total = total.reshape(n, 2, 4, 16, WIDE)
        CP[s : s + n] = total[:, 0]
        XS[s : s + n] = total[:, 1].astype(BF16)

    def swap(s, n):
        return wire(XS.at[pl.ds(s, n)], XR.at[pl.ds(s, n)], twin)

    def zput(k, p, add=None):
        s = SLOT[k]
        v = CP[s, p] + XR[s, p].astype(F32)
        if add is not None:
            v = v + ZR[add[0], add[1], p].astype(F32)
        ZW[s, p] = v.astype(BF16)
        return ZW.at[s, p]

    def zsend(way, hop, p, add=True):
        k = (4 - hop) * (1, -1)[way]
        return wire(
            zput(k, p, (way, hop - 1) if add else None),
            ZR.at[way, hop, p],
            (front, back)[way],
        )

    def zhop(hop, prev, new, pieces):
        for i in range(len(pieces)):
            for way in range(2):
                p = pieces[i] if way == 0 else 3 - pieces[i]
                prev[way][p].wait_recv()
                new[way][p] = zsend(way, hop, p)

    def text_tile(h):
        left = jnp.concatenate([SL[2 * h], SL[2 * h + 1]], axis=1)
        total = dot(left, CC[...].reshape(WIDE, WIDE), ((0,), (0,)))
        total = total.reshape(4, 4, 32, WIDE)
        TP[4 * h : 4 * h + 4] = total
        W1[4 * h : 4 * h + 4] = total.astype(BF16)

    def text_send(h):
        to = (ys, xs)[h]
        return {
            (j2, j1): wire(W1.at[4 * h + j1, j2], R1.at[h, j1 - 1, j2], to[j1])
            for j2 in (2, 1, 3, 0)
            for j1 in (2, 1, 3)
        }

    for s in range(3, 8):
        g_t[s].wait_recv()
    slopes(3, 5, (2, 3))
    for copy in a2:
        copy.wait_recv()
    slopes(3, 5, (0, 1))
    for copy in (*g_f.values(), *g_b.values()):
        copy.wait_recv()
    g_t[2] = wire(CC.at[2, 0], CC.at[2, 1], twin)
    for s in (0, 1, 2):
        g_t[s].wait_recv()
    slopes(0, 3)
    pulls(2, 1)
    x_4 = swap(2, 1)
    pulls(0, 2)
    x_3 = swap(0, 2)
    x_4.wait_recv()
    z0 = [{p: zsend(0, 0, p, False) for p in (0, 1)}, {p: zsend(1, 0, p, False) for p in (3, 2)}]
    text_tile(0)
    t1 = [text_send(0)]
    x_3.wait_recv()
    z1 = [{p: zsend(0, 1, p, False) for p in (2, 3)}, {p: zsend(1, 1, p, False) for p in (1, 0)}]
    text_tile(1)
    t1.append(text_send(1))
    pulls(3, 5)
    x_2, x_1, x_0 = swap(3, 2), swap(5, 2), swap(7, 1)
    zhop(1, z0, z1, (0, 1))

    def text_sum(h, j2):
        for j1 in (2, 1, 3):
            t1[h][j2, j1].wait_recv()
        return TP[4 * h, j2] + sum(R1[h, j, j2].astype(F32) for j in range(3))

    t2 = [{}, {}]

    def text_round(j2):
        for h in range(2):
            W2[h, j2] = text_sum(h, j2).astype(BF16)
            t2[h][j2] = wire(W2.at[h, j2], R2.at[h, j2 - 1], (xs, ys)[h][j2])

    x_2.wait_recv()
    z2 = [{}, {}]
    zhop(2, z1, z2, (2, 3, 0, 1))
    text_round(2)
    x_1.wait_recv()
    z3 = [{}, {}]
    zhop(3, z2, z3, (2, 3, 0, 1))
    text_round(1)

    x_0.wait_recv()
    for way in range(2):
        for copy in z3[way].values():
            copy.wait_recv()
    pull = CP[7] + XR[7].astype(F32) + ZR[0, 3].astype(F32) + ZR[1, 3].astype(F32)
    pull = pull.reshape(64, WIDE)
    unit = CU[...]
    radial = jnp.sum(unit * pull, axis=1, keepdims=True)
    grad = (pull - unit * radial) / CN[:, 0:1]
    for h in range(2):
        for k in range(2):
            cols = grad[:, (h * 2 + k) * 256 : (h * 2 + k + 1) * 256]
            GS[h, k] = cols
            GY[h, k] = cols.astype(BF16)
    o_y = wire(GY.at[1 - hi, c], HF.at[0], ys[2])
    o_m = wire(GY.at[1 - hi, 1 - c], HF.at[1], cross)
    o_t = wire(GS.at[hi, 1 - c], GR, twin)
    cg[hi, c] = GS[hi, c]

    text_round(3)
    text_pull = [text_sum(h, 0) for h in range(2)]
    for h in range(2):
        for copy in t2[h].values():
            copy.wait_recv()
        text_pull[h] = text_pull[h] + sum(R2[h, j].astype(F32) for j in range(3))
    text_pull = jnp.concatenate(text_pull, axis=0)
    text_unit = TU[...]
    text_radial = jnp.sum(text_unit * text_pull, axis=1, keepdims=True)
    tg[...] = (text_pull - text_unit * text_radial) / TN[:, 0:1]

    for copy in (o_t, o_y, o_m):
        copy.wait_recv()
    cg[hi, 1 - c] = GR[...]
    cg[1 - hi, c] = HF[0].astype(F32)
    cg[1 - hi, 1 - c] = HF[1].astype(F32)
    wire.drain()


def shards(cell_states, projection, text_embeds, group_ids):
    vmem = pltpu.VMEM
    scratch = [
        vmem((2, 2, 64, WIDE), BF16),
        vmem((4, WIDE, 256), BF16),
        vmem((64, WIDE), BF16),
        vmem((2, 128), I32),
        pltpu.SemaphoreType.DMA((7,)),
        vmem((8, 4, 32, WIDE), BF16),
        vmem((4, 4, 8, 128), I32),
        vmem((8, 2, 64, WIDE), BF16),
        vmem((8, 8, 128), I32),
        vmem((64, WIDE), F32),
        vmem((64, 128), F32),
        vmem((64, WIDE), F32),
        vmem((64, 128), F32),
        vmem((2, 2, 64, WIDE), F32),
        vmem((2, 64, WIDE), F32),
        vmem((64, WIDE), BF16),
        vmem((64, WIDE), BF16),
        vmem((8, 1, 128), F32),
        vmem((8, 128, 128), F32),
        vmem((4, WIDE, 256), BF16),
        vmem((8, 4, 16, WIDE), F32),
        vmem((8, 4, 16, WIDE), BF16),
        vmem((8, 4, 16, WIDE), BF16),
        vmem((8, 4, 16, WIDE), BF16),
        vmem((2, 4, 4, 16, WIDE), BF16),
        vmem((8, 4, 32, WIDE), F32),
        vmem((8, 4, 32, WIDE), BF16),
        vmem((2, 3, 4, 32, WIDE), BF16),
        vmem((2, 4, 32, WIDE), BF16),
        vmem((2, 3, 32, WIDE), BF16),
        vmem((2, 2, 64, 256), F32),
        vmem((64, 256), F32),
        vmem((2, 2, 64, 256), BF16),
        vmem((2, 64, 256), BF16),
        pltpu.SemaphoreType.DMA((COPIES,)),
        pltpu.SemaphoreType.DMA((COPIES,)),
    ]
    whole = pl.BlockSpec(memory_space=pltpu.VMEM)
    cell_grad, text_grad = pl.pallas_call(
        kernel,
        out_shape=(
            jax.ShapeDtypeStruct((2, 2, 64, 256), F32),
            jax.ShapeDtypeStruct((64, WIDE), F32),
        ),
        in_specs=[pl.BlockSpec(memory_space=pltpu.HBM)] * 4,
        out_specs=(whole, whole),
        scratch_shapes=scratch,
        compiler_params=pltpu.CompilerParams(
            collective_id=0, has_side_effects=True, vmem_limit_bytes=34 * 1024 * 1024
        ),
    )(
        pltpu.with_memory_space_constraint(cell_states.reshape(2, 2, 64, WIDE), pltpu.HBM),
        pltpu.with_memory_space_constraint(projection, pltpu.HBM),
        pltpu.with_memory_space_constraint(text_embeds, pltpu.HBM),
        pltpu.with_memory_space_constraint(group_ids.reshape(2, 128), pltpu.HBM),
    )
    return cell_grad.reshape(256, 256), text_grad


def solution(mesh):
    return jax.shard_map(
        shards,
        mesh=mesh,
        in_specs=(P("dp", "mp"), P("mp", None), P(("dp", "mp"), None), P("dp")),
        out_specs=(P("dp", "mp"), P(("dp", "mp"), None)),
        check_vma=False,
    )
```

```python
import jax
import jax.numpy as jnp
from jax import lax
from jax.experimental import pallas as pl
from jax.experimental.pallas import tpu as pltpu
from jax.sharding import PartitionSpec as P

MESH = pl.DeviceIdType.MESH
F32, BF16, I32 = jnp.float32, jnp.bfloat16, jnp.int32
WIDE = 1024
EPS = 1e-06
COPIES = 188
SLOT = {-3: 0, 3: 1, 4: 2, -4: 2, -2: 3, 2: 4, -1: 5, 1: 6, 0: 7}


class Wire:
    def __init__(self, send, recv):
        self.send, self.recv, self.open = send, recv, []

    def __call__(self, src, dst, where):
        i = len(self.open)
        copy = pltpu.make_async_remote_copy(
            src_ref=src,
            dst_ref=dst,
            send_sem=self.send.at[i],
            recv_sem=self.recv.at[i],
            device_id=where,
            device_id_type=MESH,
        )
        copy.start()
        self.open.append(copy)
        return copy

    def drain(self):
        for copy in self.open:
            copy.wait_send()


def dot(a, b, dims):
    return lax.dot_general(a, b, (dims, ((), ())), preferred_element_type=F32)


def kernel(
    cs_hbm, pj_hbm, te_hbm, ids_hbm, cg, tg,
    cs, pj, te, ids, load,
    T, TI, CC, CI, CU, CN, TU, TN, PO, PR, QS, FN,
    IDR, IDC, SL, CP, XS, XR, ZW, ZR,
    TP, W1, RO, RN, W2, R2, GS, GR, GY, HF,
    send, recv,
):
    dp, mp = lax.axis_index("dp"), lax.axis_index("mp")
    x, z, ylo = dp // 16, lax.rem(dp // 2, 8), lax.rem(dp, 2)
    hi, c = mp // 2, lax.rem(mp, 2)
    y = hi * 2 + ylo

    def dev(x, y, z, c):
        return ((x * 8 + z) * 2 + lax.rem(y, 2), (y // 2) * 2 + c)

    xs = [dev(lax.rem(x + k, 4), y, z, c) for k in range(4)]
    ys = [dev(x, lax.rem(y + k, 4), z, c) for k in range(4)]
    zs = [dev(x, y, lax.rem(z + k, 8), c) for k in range(8)]
    front, back = zs[1], zs[7]
    twin, cross = dev(x, y, z, 1 - c), dev(x, lax.rem(y + 2, 4), z, 1 - c)

    loads = [
        pltpu.make_async_copy(te_hbm, te, load.at[0]),
        pltpu.make_async_copy(ids_hbm, ids, load.at[1]),
        pltpu.make_async_copy(cs_hbm, cs, load.at[2]),
    ]
    for n in range(4):
        cols = pl.ds(n * 256, 256)
        loads.append(pltpu.make_async_copy(pj_hbm.at[:, cols], pj.at[n], load.at[3 + n]))
    for copy in loads:
        copy.start()

    barrier = pltpu.get_barrier_semaphore()
    peers = (*xs[1:], *ys[1:], *zs[1:], twin, cross)
    for where in peers:
        pl.semaphore_signal(barrier, inc=1, device_id=where, device_id_type=MESH)
    wire = Wire(send, recv)

    loads[1].wait()
    row = jnp.where(hi == 0, ids[0:1, :], ids[1:2, :])
    row = jnp.where(c == 0, row, jnp.roll(row, 64, axis=1))
    TI[0, 0] = jnp.broadcast_to(row, (8, 128))
    CI[0] = jnp.broadcast_to(row, (8, 128))

    loads[0].wait()
    text = te[...].astype(F32)
    text_norm = jnp.sqrt(jnp.sum(text * text, axis=1, keepdims=True) + EPS)
    text_unit = text / text_norm
    TU[...] = text_unit
    TN[...] = jnp.broadcast_to(text_norm, (64, 128))
    half = text_unit.astype(BF16)
    T[0, 0] = half[0:32]
    T[4, 0] = half[32:64]

    loads[2].wait()
    rows = cs[...].reshape(256, WIDE)
    for n in range(4):
        cols = pl.ds(n * 256, 256)
        loads[3 + n].wait()
        part = dot(rows, pj[n], ((1,), (0,))).reshape(2, 2, 64, 256)
        PO[0, :, :, cols] = part[:, 0]
        PO[1, :, :, cols] = part[:, 1]
    pl.semaphore_wait(barrier, len(peers))
    p_q = wire(PO.at[1 - c, 1 - hi], PR.at[0], twin)
    p_o = wire(PO.at[1 - c, hi], PR.at[1], twin)

    def spread(h, block):
        to = (ys, xs)[h]
        return [
            wire(T.at[4 * h, block], T.at[4 * h + 4 - k, block], to[k]) for k in (1, 3, 2)
        ]

    a1 = {4 - k: wire(T.at[0, 0], T.at[0, 4 - k], xs[k]) for k in (1, 3)}
    b1 = {4 - k: wire(T.at[4, 0], T.at[4, 4 - k], ys[k]) for k in (1, 3)}
    a1[2] = wire(T.at[0, 0], T.at[0, 2], xs[2])
    ix = [wire(TI.at[0, 0], TI.at[0, 4 - k], xs[k]) for k in range(1, 4)]
    iz = [wire(CI.at[0], CI.at[8 - k], zs[k]) for k in range(1, 8)]
    b2 = spread(1, 0)

    p_q.wait_recv()
    away = (PO[c, 1 - hi] + PR[0]).astype(BF16)
    QS[0] = jnp.concatenate([away[0:16], away[48:64]], axis=0)
    QS[1] = away[16:48]
    q = [wire(QS.at[k], FN.at[k], ys[2]) for k in range(2)]
    b1[2] = wire(T.at[4, 0], T.at[4, 2], ys[2])
    a2 = spread(0, 0)
    p_o.wait_recv()
    PR[1] = PO[c, hi] + PR[1]

    for block in (3, 1):
        b1[block].wait_recv()
        b2 += spread(1, block)
    for block in (3, 1, 2):
        a1[block].wait_recv()
        a2 += spread(0, block)
    for copy in ix:
        copy.wait_recv()
    iy = [wire(TI.at[0], TI.at[4 - k], ys[k]) for k in (2, 1, 3)]

    def piece(p):
        return pl.ds(16 * p, 16)

    def pass_on(k, p, step, where):
        return wire(
            CC.at[SLOT[k], 0, piece(p)], CC.at[SLOT[k + step], 0, piece(p)], where
        )

    def cell_rows(k, pieces):
        q[k].wait_recv()
        own = jnp.concatenate([PR[1, piece(p)] for p in pieces], axis=0)
        emb = own + FN[k].astype(F32)
        norm = jnp.sqrt(jnp.sum(emb * emb, axis=1, keepdims=True) + EPS)
        unit = emb / norm
        norm = jnp.broadcast_to(norm, (32, 128))
        for i, p in enumerate(pieces):
            CU[piece(p)] = unit[16 * i : 16 * i + 16]
            CN[piece(p)] = norm[16 * i : 16 * i + 16]
            CC[7, 0, piece(p)] = unit[16 * i : 16 * i + 16].astype(BF16)

    cell_rows(0, (0, 3))
    g_f, g_b = {0: pass_on(0, 0, -1, front)}, {3: pass_on(0, 3, 1, back)}
    cell_rows(1, (1, 2))
    for p in range(1, 4):
        g_f[p] = pass_on(0, p, -1, front)
        g_b[3 - p] = pass_on(0, 3 - p, 1, back)
    g_t = {7: wire(CC.at[7, 0], CC.at[7, 1], twin)}
    b1[2].wait_recv()
    b2 += spread(1, 2)
    for k in range(1, 4):
        n_f, n_b = {}, {}
        for p in range(4):
            g_f[p].wait_recv()
            if k < 3 or p < 2:
                n_f[p] = pass_on(-k, p, -1, front)
            g_b[3 - p].wait_recv()
            if k < 3 or p < 2:
                n_b[3 - p] = pass_on(k, 3 - p, 1, back)
        g_f, g_b = n_f, n_b
        for s in (SLOT[-k], SLOT[k]):
            g_t[s] = wire(CC.at[s, 0], CC.at[s, 1], twin)

    for copy in (*iy, *iz):
        copy.wait_recv()
    lane = lax.broadcasted_iota(I32, (1, 128), 1)
    for h in range(2):
        for a in range(4):
            parts = [TI[a, b, 0:1] if h == 0 else TI[b, a, 0:1] for b in range(4)]
            names = jnp.zeros((1, 128), I32)
            for b in range(4):
                moved = parts[b]
                if (b - h) % 4:
                    moved = jnp.roll(moved, 32 * ((b - h) % 4), axis=1)
                names = jnp.where(lane // 32 == b, moved, names)
            IDR[h * 4 + a] = names.astype(F32)
    for k, s in SLOT.items():
        if k != -4:
            IDC[s] = jnp.broadcast_to(CI[k % 8, 0:1, :].astype(F32), (128, 128)).T
    for copy in b2:
        copy.wait_recv()

    def slopes(s, n, tiles=(2, 3, 0, 1)):
        rows = n * 128
        cells = CC[s : s + n].reshape(rows, WIDE)
        col = IDC[s : s + n].reshape(rows, 128)
        col = jnp.concatenate([col, col], axis=1)
        for t in tiles:
            inner = dot(cells, T[2 * t : 2 * t + 2].reshape(256, WIDE), ((1,), (1,)))
            names = jnp.concatenate([IDR[t * 2], IDR[t * 2 + 1]], axis=1)
            slope = 5.0 * jnp.tanh(5.0 * inner - 2.0) + jnp.where(col == names, -5.0, 5.0)
            SL[t, s * 128 : s * 128 + rows, :] = slope.astype(BF16)

    def pulls(s, n):
        rows = n * 128
        left = [SL[t, s * 128 : s * 128 + rows, :] for t in range(4)]
        total = dot(jnp.concatenate(left, axis=1), T[...].reshape(WIDE, WIDE), ((1,), (0,)))
        total = total.reshape(n, 2, 4, 16, WIDE)
        CP[s : s + n] = total[:, 0]
        XS[s : s + n] = total[:, 1].astype(BF16)

    def swap(s, n):
        return wire(XS.at[pl.ds(s, n)], XR.at[pl.ds(s, n)], twin)

    def zput(k, p, add=None):
        s = SLOT[k]
        v = CP[s, p] + XR[s, p].astype(F32)
        if add is not None:
            v = v + ZR[add[0], add[1], p].astype(F32)
        ZW[s, p] = v.astype(BF16)
        return ZW.at[s, p]

    def zsend(way, hop, p, add=True):
        k = (4 - hop) * (1, -1)[way]
        return wire(
            zput(k, p, (way, hop - 1) if add else None),
            ZR.at[way, hop, p],
            (front, back)[way],
        )

    def zhop(hop, prev, new, pieces):
        for i in range(len(pieces)):
            for way in range(2):
                p = pieces[i] if way == 0 else 3 - pieces[i]
                prev[way][p].wait_recv()
                new[way][p] = zsend(way, hop, p)

    def text_tile(h):
        left = jnp.concatenate([SL[2 * h], SL[2 * h + 1]], axis=1)
        total = dot(left, CC[...].reshape(WIDE, WIDE), ((0,), (0,)))
        total = total.reshape(4, 4, 32, WIDE)
        TP[4 * h : 4 * h + 4] = total
        W1[4 * h : 4 * h + 4] = total.astype(BF16)

    low, high = pl.ds(0, 16), pl.ds(16, 16)
    blocks = (2, 1, 3, 0)

    def text_send(h):
        to = (ys, xs)[h]
        for j in blocks:
            over[h][0, j] = wire(W1.at[4 * h + 2, j, low], RO.at[h, 0, j], to[1])
            over[h][1, j] = wire(W1.at[4 * h + 2, j, high], RO.at[h, 1, j], to[3])
        for j in blocks:
            near[h][0, 1, j] = wire(W1.at[4 * h + 1, j, high], RN.at[h, 0, j, high], to[1])
            near[h][1, 0, j] = wire(W1.at[4 * h + 3, j, low], RN.at[h, 1, j, low], to[3])

    def text_add(h):
        to = (ys, xs)[h]
        for j in blocks:
            over[h][0, j].wait_recv()
            v = TP[4 * h + 1, j, low] + RO[h, 0, j].astype(F32)
            W1[4 * h + 1, j, low] = v.astype(BF16)
            near[h][0, 0, j] = wire(W1.at[4 * h + 1, j, low], RN.at[h, 0, j, low], to[1])
            over[h][1, j].wait_recv()
            v = TP[4 * h + 3, j, high] + RO[h, 1, j].astype(F32)
            W1[4 * h + 3, j, high] = v.astype(BF16)
            near[h][1, 1, j] = wire(W1.at[4 * h + 3, j, high], RN.at[h, 1, j, high], to[3])

    over, near = [{}, {}], [{}, {}]
    for s in range(3, 8):
        g_t[s].wait_recv()
    slopes(3, 5, (2, 3))
    for copy in a2:
        copy.wait_recv()
    slopes(3, 5, (0, 1))
    for copy in (*g_f.values(), *g_b.values()):
        copy.wait_recv()
    g_t[2] = wire(CC.at[2, 0], CC.at[2, 1], twin)
    for s in (0, 1, 2):
        g_t[s].wait_recv()
    slopes(0, 3)
    pulls(2, 1)
    x_4 = swap(2, 1)
    pulls(0, 2)
    x_3 = swap(0, 2)
    x_4.wait_recv()
    z0 = [{p: zsend(0, 0, p, False) for p in (0, 1)}, {p: zsend(1, 0, p, False) for p in (3, 2)}]
    text_tile(0)
    text_send(0)
    x_3.wait_recv()
    z1 = [{p: zsend(0, 1, p, False) for p in (2, 3)}, {p: zsend(1, 1, p, False) for p in (1, 0)}]
    text_tile(1)
    text_send(1)
    pulls(3, 5)
    x_2, x_1, x_0 = swap(3, 2), swap(5, 2), swap(7, 1)
    zhop(1, z0, z1, (0, 1))
    text_add(0)

    def text_sum(h, j2):
        for way in range(2):
            for part in range(2):
                near[h][way, part, j2].wait_recv()
        return TP[4 * h, j2] + RN[h, 0, j2].astype(F32) + RN[h, 1, j2].astype(F32)

    t2 = [{}, {}]

    def text_round(j2):
        for h in range(2):
            W2[h, j2] = text_sum(h, j2).astype(BF16)
            t2[h][j2] = wire(W2.at[h, j2], R2.at[h, j2 - 1], (xs, ys)[h][j2])

    x_2.wait_recv()
    z2 = [{}, {}]
    zhop(2, z1, z2, (2, 3, 0, 1))
    text_add(1)
    x_1.wait_recv()
    z3 = [{}, {}]
    zhop(3, z2, z3, (2, 3, 0, 1))
    text_round(2)
    text_round(1)
    text_round(3)

    x_0.wait_recv()
    o_y, o_m, o_t = [], [], []
    for part, pieces in enumerate(((0, 3), (1, 2))):
        for p in pieces:
            for way in range(2):
                z3[way][p].wait_recv()
        pull = jnp.concatenate(
            [
                CP[7, p]
                + XR[7, p].astype(F32)
                + ZR[0, 3, p].astype(F32)
                + ZR[1, 3, p].astype(F32)
                for p in pieces
            ],
            axis=0,
        )
        unit = jnp.concatenate([CU[piece(p)] for p in pieces], axis=0)
        norm = jnp.concatenate([CN[piece(p)] for p in pieces], axis=0)[:, 0:1]
        radial = jnp.sum(unit * pull, axis=1, keepdims=True)
        grad = (pull - unit * radial) / norm
        for h in range(2):
            for k in range(2):
                cols = grad[:, (h * 2 + k) * 256 : (h * 2 + k + 1) * 256]
                GS[part, h, k] = cols
                GY[part, h, k] = cols.astype(BF16)
        o_y.append(wire(GY.at[part, 1 - hi, c], HF.at[part, 0], ys[2]))
        o_m.append(wire(GY.at[part, 1 - hi, 1 - c], HF.at[part, 1], cross))
        o_t.append(wire(GS.at[part, hi, 1 - c], GR.at[part], twin))
        for i, p in enumerate(pieces):
            cg[hi, c, piece(p)] = GS[part, hi, c, piece(i)]

    text_pull = [text_sum(h, 0) for h in range(2)]
    for h in range(2):
        for copy in t2[h].values():
            copy.wait_recv()
        text_pull[h] = text_pull[h] + sum(R2[h, j].astype(F32) for j in range(3))
    text_pull = jnp.concatenate(text_pull, axis=0)
    text_unit = TU[...]
    text_radial = jnp.sum(text_unit * text_pull, axis=1, keepdims=True)
    tg[...] = (text_pull - text_unit * text_radial) / TN[:, 0:1]

    wire.drain()
    for part, pieces in enumerate(((0, 3), (1, 2))):
        for copy in (o_t[part], o_y[part], o_m[part]):
            copy.wait_recv()
        for i, p in enumerate(pieces):
            cg[hi, 1 - c, piece(p)] = GR[part, piece(i)]
            cg[1 - hi, c, piece(p)] = HF[part, 0, piece(i)].astype(F32)
            cg[1 - hi, 1 - c, piece(p)] = HF[part, 1, piece(i)].astype(F32)


def shards(cell_states, projection, text_embeds, group_ids):
    vmem = pltpu.VMEM
    scratch = [
        vmem((2, 2, 64, WIDE), BF16),
        vmem((4, WIDE, 256), BF16),
        vmem((64, WIDE), BF16),
        vmem((2, 128), I32),
        pltpu.SemaphoreType.DMA((7,)),
        vmem((8, 4, 32, WIDE), BF16),
        vmem((4, 4, 8, 128), I32),
        vmem((8, 2, 64, WIDE), BF16),
        vmem((8, 8, 128), I32),
        vmem((64, WIDE), F32),
        vmem((64, 128), F32),
        vmem((64, WIDE), F32),
        vmem((64, 128), F32),
        vmem((2, 2, 64, WIDE), F32),
        vmem((2, 64, WIDE), F32),
        vmem((2, 32, WIDE), BF16),
        vmem((2, 32, WIDE), BF16),
        vmem((8, 1, 128), F32),
        vmem((8, 128, 128), F32),
        vmem((4, WIDE, 256), BF16),
        vmem((8, 4, 16, WIDE), F32),
        vmem((8, 4, 16, WIDE), BF16),
        vmem((8, 4, 16, WIDE), BF16),
        vmem((8, 4, 16, WIDE), BF16),
        vmem((2, 4, 4, 16, WIDE), BF16),
        vmem((8, 4, 32, WIDE), F32),
        vmem((8, 4, 32, WIDE), BF16),
        vmem((2, 2, 4, 16, WIDE), BF16),
        vmem((2, 2, 4, 32, WIDE), BF16),
        vmem((2, 4, 32, WIDE), BF16),
        vmem((2, 3, 32, WIDE), BF16),
        vmem((2, 2, 2, 32, 256), F32),
        vmem((2, 32, 256), F32),
        vmem((2, 2, 2, 32, 256), BF16),
        vmem((2, 2, 32, 256), BF16),
        pltpu.SemaphoreType.DMA((COPIES,)),
        pltpu.SemaphoreType.DMA((COPIES,)),
    ]
    whole = pl.BlockSpec(memory_space=pltpu.VMEM)
    cell_grad, text_grad = pl.pallas_call(
        kernel,
        out_shape=(
            jax.ShapeDtypeStruct((2, 2, 64, 256), F32),
            jax.ShapeDtypeStruct((64, WIDE), F32),
        ),
        in_specs=[pl.BlockSpec(memory_space=pltpu.HBM)] * 4,
        out_specs=(whole, whole),
        scratch_shapes=scratch,
        compiler_params=pltpu.CompilerParams(
            collective_id=0, has_side_effects=True, vmem_limit_bytes=34 * 1024 * 1024
        ),
    )(
        pltpu.with_memory_space_constraint(cell_states.reshape(2, 2, 64, WIDE), pltpu.HBM),
        pltpu.with_memory_space_constraint(projection, pltpu.HBM),
        pltpu.with_memory_space_constraint(text_embeds, pltpu.HBM),
        pltpu.with_memory_space_constraint(group_ids.reshape(2, 128), pltpu.HBM),
    )
    return cell_grad.reshape(256, 256), text_grad


def solution(mesh):
    return jax.shard_map(
        shards,
        mesh=mesh,
        in_specs=(P("dp", "mp"), P("mp", None), P(("dp", "mp"), None), P("dp")),
        out_specs=(P("dp", "mp"), P(("dp", "mp"), None)),
        check_vma=False,
    )
```

```python
import jax
import jax.numpy as jnp
from jax import lax
from jax.experimental import pallas as pl
from jax.experimental.pallas import tpu as pltpu
from jax.sharding import PartitionSpec as P

MESH = pl.DeviceIdType.MESH
F32, BF16, I32 = jnp.float32, jnp.bfloat16, jnp.int32
WIDE = 1024
EPS = 1e-06
COPIES = 188
SLOT = {-3: 0, 3: 1, 4: 2, -4: 2, -2: 3, 2: 4, -1: 5, 1: 6, 0: 7}


class Wire:
    def __init__(self, send, recv):
        self.send, self.recv, self.open = send, recv, []

    def __call__(self, src, dst, where):
        i = len(self.open)
        copy = pltpu.make_async_remote_copy(
            src_ref=src,
            dst_ref=dst,
            send_sem=self.send.at[i],
            recv_sem=self.recv.at[i],
            device_id=where,
            device_id_type=MESH,
        )
        copy.start()
        self.open.append(copy)
        return copy

    def drain(self):
        for copy in self.open:
            copy.wait_send()


def dot(a, b, dims):
    return lax.dot_general(a, b, (dims, ((), ())), preferred_element_type=F32)


def kernel(
    cs_hbm, pj_hbm, te_hbm, ids_hbm, cg, tg,
    cs, pj, te, ids, load,
    T, TI, CC, CI, CU, CN, TU, TN, PO, PR, QS, FN,
    IDR, IDC, SL, CP, XS, XR, ZW, ZR,
    TP, W1, RO, RN, W2, R2, GS, GR, GY, HF,
    send, recv,
):
    dp, mp = lax.axis_index("dp"), lax.axis_index("mp")
    x, z, ylo = dp // 16, lax.rem(dp // 2, 8), lax.rem(dp, 2)
    hi, c = mp // 2, lax.rem(mp, 2)
    y = hi * 2 + ylo

    def dev(x, y, z, c):
        return ((x * 8 + z) * 2 + lax.rem(y, 2), (y // 2) * 2 + c)

    xs = [dev(lax.rem(x + k, 4), y, z, c) for k in range(4)]
    ys = [dev(x, lax.rem(y + k, 4), z, c) for k in range(4)]
    zs = [dev(x, y, lax.rem(z + k, 8), c) for k in range(8)]
    front, back = zs[1], zs[7]
    twin, cross = dev(x, y, z, 1 - c), dev(x, lax.rem(y + 2, 4), z, 1 - c)

    loads = [
        pltpu.make_async_copy(te_hbm, te, load.at[0]),
        pltpu.make_async_copy(ids_hbm, ids, load.at[1]),
        pltpu.make_async_copy(cs_hbm, cs, load.at[2]),
    ]
    for n in range(4):
        cols = pl.ds(n * 256, 256)
        loads.append(pltpu.make_async_copy(pj_hbm.at[:, cols], pj.at[n], load.at[3 + n]))
    for copy in loads:
        copy.start()

    barrier = pltpu.get_barrier_semaphore()
    peers = (*xs[1:], *ys[1:], *zs[1:], twin, cross)
    for where in peers:
        pl.semaphore_signal(barrier, inc=1, device_id=where, device_id_type=MESH)
    wire = Wire(send, recv)

    loads[1].wait()
    row = jnp.where(hi == 0, ids[0:1, :], ids[1:2, :])
    row = jnp.where(c == 0, row, jnp.roll(row, 64, axis=1))
    TI[0, 0] = jnp.broadcast_to(row, (8, 128))
    CI[0] = jnp.broadcast_to(row, (8, 128))

    loads[0].wait()
    text = te[...].astype(F32)
    text_norm = jnp.sqrt(jnp.sum(text * text, axis=1, keepdims=True) + EPS)
    text_unit = text / text_norm
    TU[...] = text_unit
    TN[...] = jnp.broadcast_to(text_norm, (64, 128))
    half = text_unit.astype(BF16)
    T[0, 0] = half[0:32]
    T[4, 0] = half[32:64]

    loads[2].wait()
    rows = cs[...].reshape(256, WIDE)
    for n in range(4):
        cols = pl.ds(n * 256, 256)
        loads[3 + n].wait()
        part = dot(rows, pj[n], ((1,), (0,))).reshape(2, 2, 64, 256)
        PO[0, :, :, cols] = part[:, 0]
        PO[1, :, :, cols] = part[:, 1]
    pl.semaphore_wait(barrier, len(peers))
    p_q = wire(PO.at[1 - c, 1 - hi], PR.at[0], twin)
    p_o = wire(PO.at[1 - c, hi], PR.at[1], twin)

    def spread(h, block):
        to = (ys, xs)[h]
        return [
            wire(T.at[4 * h, block], T.at[4 * h + 4 - k, block], to[k]) for k in (1, 3, 2)
        ]

    ix = [wire(TI.at[0, 0], TI.at[0, 4 - k], xs[k]) for k in range(1, 4)]
    iz = [wire(CI.at[0], CI.at[8 - k], zs[k]) for k in range(1, 8)]
    a1 = {4 - k: wire(T.at[0, 0], T.at[0, 4 - k], xs[k]) for k in (1, 3)}
    b1 = {4 - k: wire(T.at[4, 0], T.at[4, 4 - k], ys[k]) for k in (1, 3)}
    a1[2] = wire(T.at[0, 0], T.at[0, 2], xs[2])
    b2 = spread(1, 0)

    p_q.wait_recv()
    away = (PO[c, 1 - hi] + PR[0]).astype(BF16)
    QS[0] = jnp.concatenate([away[0:16], away[48:64]], axis=0)
    QS[1] = away[16:48]
    q = [wire(QS.at[k], FN.at[k], ys[2]) for k in range(2)]
    b1[2] = wire(T.at[4, 0], T.at[4, 2], ys[2])
    a2 = spread(0, 0)
    p_o.wait_recv()
    PR[1] = PO[c, hi] + PR[1]

    for copy in ix:
        copy.wait_recv()
    iy = [wire(TI.at[0], TI.at[4 - k], ys[k]) for k in (2, 1, 3)]
    for block in (3, 1):
        b1[block].wait_recv()
        b2 += spread(1, block)
    for block in (3, 1, 2):
        a1[block].wait_recv()
        a2 += spread(0, block)

    def piece(p):
        return pl.ds(16 * p, 16)

    def pass_on(k, p, step, where):
        return wire(
            CC.at[SLOT[k], 0, piece(p)], CC.at[SLOT[k + step], 0, piece(p)], where
        )

    def cell_rows(k, pieces):
        q[k].wait_recv()
        own = jnp.concatenate([PR[1, piece(p)] for p in pieces], axis=0)
        emb = own + FN[k].astype(F32)
        norm = jnp.sqrt(jnp.sum(emb * emb, axis=1, keepdims=True) + EPS)
        unit = emb / norm
        norm = jnp.broadcast_to(norm, (32, 128))
        for i, p in enumerate(pieces):
            CU[piece(p)] = unit[16 * i : 16 * i + 16]
            CN[piece(p)] = norm[16 * i : 16 * i + 16]
            CC[7, 0, piece(p)] = unit[16 * i : 16 * i + 16].astype(BF16)

    cell_rows(0, (0, 3))
    g_f, g_b = {0: pass_on(0, 0, -1, front)}, {3: pass_on(0, 3, 1, back)}
    cell_rows(1, (1, 2))
    for p in range(1, 4):
        g_f[p] = pass_on(0, p, -1, front)
        g_b[3 - p] = pass_on(0, 3 - p, 1, back)
    g_t = {7: wire(CC.at[7, 0], CC.at[7, 1], twin)}
    b1[2].wait_recv()
    b2 += spread(1, 2)
    def names_of_all():
        for copy in (*iy, *iz):
            copy.wait_recv()
        lane = lax.broadcasted_iota(I32, (1, 128), 1)
        for h in range(2):
            for a in range(4):
                parts = [TI[a, b, 0:1] if h == 0 else TI[b, a, 0:1] for b in range(4)]
                names = jnp.zeros((1, 128), I32)
                for b in range(4):
                    moved = parts[b]
                    if (b - h) % 4:
                        moved = jnp.roll(moved, 32 * ((b - h) % 4), axis=1)
                    names = jnp.where(lane // 32 == b, moved, names)
                IDR[h * 4 + a] = names.astype(F32)
        for k, s in SLOT.items():
            if k != -4:
                IDC[s] = jnp.broadcast_to(CI[k % 8, 0:1, :].astype(F32), (128, 128)).T

    for k in range(1, 4):
        n_f, n_b = {}, {}
        for p in range(4):
            g_f[p].wait_recv()
            if k < 3 or p < 2:
                n_f[p] = pass_on(-k, p, -1, front)
            g_b[3 - p].wait_recv()
            if k < 3 or p < 2:
                n_b[3 - p] = pass_on(k, 3 - p, 1, back)
        g_f, g_b = n_f, n_b
        for s in (SLOT[-k], SLOT[k]):
            g_t[s] = wire(CC.at[s, 0], CC.at[s, 1], twin)
        if k == 1:
            names_of_all()

    for copy in b2:
        copy.wait_recv()

    def slopes(s, n, tiles=(2, 3, 0, 1)):
        rows = n * 128
        cells = CC[s : s + n].reshape(rows, WIDE)
        col = IDC[s : s + n].reshape(rows, 128)
        col = jnp.concatenate([col, col], axis=1)
        for t in tiles:
            inner = dot(cells, T[2 * t : 2 * t + 2].reshape(256, WIDE), ((1,), (1,)))
            names = jnp.concatenate([IDR[t * 2], IDR[t * 2 + 1]], axis=1)
            slope = 5.0 * jnp.tanh(5.0 * inner - 2.0) + jnp.where(col == names, -5.0, 5.0)
            SL[t, s * 128 : s * 128 + rows, :] = slope.astype(BF16)

    def pulls(s, n):
        rows = n * 128
        left = [SL[t, s * 128 : s * 128 + rows, :] for t in range(4)]
        total = dot(jnp.concatenate(left, axis=1), T[...].reshape(WIDE, WIDE), ((1,), (0,)))
        total = total.reshape(n, 2, 4, 16, WIDE)
        CP[s : s + n] = total[:, 0]
        XS[s : s + n] = total[:, 1].astype(BF16)

    def swap(s, n):
        return wire(XS.at[pl.ds(s, n)], XR.at[pl.ds(s, n)], twin)

    def zput(k, p, add=None):
        s = SLOT[k]
        v = CP[s, p] + XR[s, p].astype(F32)
        if add is not None:
            v = v + ZR[add[0], add[1], p].astype(F32)
        ZW[s, p] = v.astype(BF16)
        return ZW.at[s, p]

    def zsend(way, hop, p, add=True):
        k = (4 - hop) * (1, -1)[way]
        return wire(
            zput(k, p, (way, hop - 1) if add else None),
            ZR.at[way, hop, p],
            (front, back)[way],
        )

    def zhop(hop, prev, new, pieces):
        for i in range(len(pieces)):
            for way in range(2):
                p = pieces[i] if way == 0 else 3 - pieces[i]
                prev[way][p].wait_recv()
                new[way][p] = zsend(way, hop, p)

    def text_tile(h):
        left = jnp.concatenate([SL[2 * h], SL[2 * h + 1]], axis=1)
        total = dot(left, CC[...].reshape(WIDE, WIDE), ((0,), (0,)))
        total = total.reshape(4, 4, 32, WIDE)
        TP[4 * h : 4 * h + 4] = total
        W1[4 * h : 4 * h + 4] = total.astype(BF16)

    low, high = pl.ds(0, 16), pl.ds(16, 16)
    blocks = (2, 1, 3, 0)

    def text_send(h):
        to = (ys, xs)[h]
        for j in blocks:
            over[h][0, j] = wire(W1.at[4 * h + 2, j, low], RO.at[h, 0, j], to[1])
            over[h][1, j] = wire(W1.at[4 * h + 2, j, high], RO.at[h, 1, j], to[3])
        for j in blocks:
            near[h][0, 1, j] = wire(W1.at[4 * h + 1, j, high], RN.at[h, 0, j, high], to[1])
            near[h][1, 0, j] = wire(W1.at[4 * h + 3, j, low], RN.at[h, 1, j, low], to[3])

    def text_add(h):
        to = (ys, xs)[h]
        for j in blocks:
            over[h][0, j].wait_recv()
            v = TP[4 * h + 1, j, low] + RO[h, 0, j].astype(F32)
            W1[4 * h + 1, j, low] = v.astype(BF16)
            near[h][0, 0, j] = wire(W1.at[4 * h + 1, j, low], RN.at[h, 0, j, low], to[1])
            over[h][1, j].wait_recv()
            v = TP[4 * h + 3, j, high] + RO[h, 1, j].astype(F32)
            W1[4 * h + 3, j, high] = v.astype(BF16)
            near[h][1, 1, j] = wire(W1.at[4 * h + 3, j, high], RN.at[h, 1, j, high], to[3])

    over, near = [{}, {}], [{}, {}]
    for s in range(3, 8):
        g_t[s].wait_recv()
    slopes(3, 5, (2, 3))
    for copy in a2:
        copy.wait_recv()
    for copy in (*g_f.values(), *g_b.values()):
        copy.wait_recv()
    g_t[2] = wire(CC.at[2, 0], CC.at[2, 1], twin)
    slopes(3, 5, (0, 1))
    for s in (0, 1, 2):
        g_t[s].wait_recv()
    slopes(0, 3)
    pulls(2, 1)
    x_4 = swap(2, 1)
    pulls(0, 2)
    x_3 = swap(0, 2)
    x_4.wait_recv()
    z0 = [{p: zsend(0, 0, p, False) for p in (0, 1)}, {p: zsend(1, 0, p, False) for p in (3, 2)}]
    text_tile(0)
    text_send(0)
    x_3.wait_recv()
    z1 = [{p: zsend(0, 1, p, False) for p in (2, 3)}, {p: zsend(1, 1, p, False) for p in (1, 0)}]
    text_tile(1)
    text_send(1)
    pulls(3, 5)
    x_2, x_1, x_0 = swap(3, 2), swap(5, 2), swap(7, 1)
    zhop(1, z0, z1, (0, 1))
    text_add(0)

    def text_sum(h, j2):
        for way in range(2):
            for part in range(2):
                near[h][way, part, j2].wait_recv()
        return TP[4 * h, j2] + RN[h, 0, j2].astype(F32) + RN[h, 1, j2].astype(F32)

    t2 = [{}, {}]

    def text_round(j2):
        for h in range(2):
            W2[h, j2] = text_sum(h, j2).astype(BF16)
            t2[h][j2] = wire(W2.at[h, j2], R2.at[h, j2 - 1], (xs, ys)[h][j2])

    x_2.wait_recv()
    z2 = [{}, {}]
    zhop(2, z1, z2, (2, 3, 0, 1))
    text_add(1)
    x_1.wait_recv()
    z3 = [{}, {}]
    zhop(3, z2, z3, (2, 3, 0, 1))
    text_round(2)
    text_round(1)
    text_round(3)

    x_0.wait_recv()
    o_y, o_m, o_t = [], [], []
    for part, pieces in enumerate(((0, 3), (1, 2))):
        for p in pieces:
            for way in range(2):
                z3[way][p].wait_recv()
        pull = jnp.concatenate(
            [
                CP[7, p]
                + XR[7, p].astype(F32)
                + ZR[0, 3, p].astype(F32)
                + ZR[1, 3, p].astype(F32)
                for p in pieces
            ],
            axis=0,
        )
        unit = jnp.concatenate([CU[piece(p)] for p in pieces], axis=0)
        norm = jnp.concatenate([CN[piece(p)] for p in pieces], axis=0)[:, 0:1]
        radial = jnp.sum(unit * pull, axis=1, keepdims=True)
        grad = (pull - unit * radial) / norm
        for h in range(2):
            for k in range(2):
                cols = grad[:, (h * 2 + k) * 256 : (h * 2 + k + 1) * 256]
                GS[part, h, k] = cols
                GY[part, h, k] = cols.astype(BF16)
        o_y.append(wire(GY.at[part, 1 - hi, c], HF.at[part, 0], ys[2]))
        o_m.append(wire(GY.at[part, 1 - hi, 1 - c], HF.at[part, 1], cross))
        o_t.append(wire(GS.at[part, hi, 1 - c], GR.at[part], twin))
        for i, p in enumerate(pieces):
            cg[hi, c, piece(p)] = GS[part, hi, c, piece(i)]

    text_pull = [text_sum(h, 0) for h in range(2)]
    for h in range(2):
        for copy in t2[h].values():
            copy.wait_recv()
        text_pull[h] = text_pull[h] + sum(R2[h, j].astype(F32) for j in range(3))
    text_pull = jnp.concatenate(text_pull, axis=0)
    text_unit = TU[...]
    text_radial = jnp.sum(text_unit * text_pull, axis=1, keepdims=True)
    tg[...] = (text_pull - text_unit * text_radial) / TN[:, 0:1]

    wire.drain()
    for part, pieces in enumerate(((0, 3), (1, 2))):
        for copy in (o_t[part], o_y[part], o_m[part]):
            copy.wait_recv()
        for i, p in enumerate(pieces):
            cg[hi, 1 - c, piece(p)] = GR[part, piece(i)]
            cg[1 - hi, c, piece(p)] = HF[part, 0, piece(i)].astype(F32)
            cg[1 - hi, 1 - c, piece(p)] = HF[part, 1, piece(i)].astype(F32)


def shards(cell_states, projection, text_embeds, group_ids):
    vmem = pltpu.VMEM
    scratch = [
        vmem((2, 2, 64, WIDE), BF16),
        vmem((4, WIDE, 256), BF16),
        vmem((64, WIDE), BF16),
        vmem((2, 128), I32),
        pltpu.SemaphoreType.DMA((7,)),
        vmem((8, 4, 32, WIDE), BF16),
        vmem((4, 4, 8, 128), I32),
        vmem((8, 2, 64, WIDE), BF16),
        vmem((8, 8, 128), I32),
        vmem((64, WIDE), F32),
        vmem((64, 128), F32),
        vmem((64, WIDE), F32),
        vmem((64, 128), F32),
        vmem((2, 2, 64, WIDE), F32),
        vmem((2, 64, WIDE), F32),
        vmem((2, 32, WIDE), BF16),
        vmem((2, 32, WIDE), BF16),
        vmem((8, 1, 128), F32),
        vmem((8, 128, 128), F32),
        vmem((4, WIDE, 256), BF16),
        vmem((8, 4, 16, WIDE), F32),
        vmem((8, 4, 16, WIDE), BF16),
        vmem((8, 4, 16, WIDE), BF16),
        vmem((8, 4, 16, WIDE), BF16),
        vmem((2, 4, 4, 16, WIDE), BF16),
        vmem((8, 4, 32, WIDE), F32),
        vmem((8, 4, 32, WIDE), BF16),
        vmem((2, 2, 4, 16, WIDE), BF16),
        vmem((2, 2, 4, 32, WIDE), BF16),
        vmem((2, 4, 32, WIDE), BF16),
        vmem((2, 3, 32, WIDE), BF16),
        vmem((2, 2, 2, 32, 256), F32),
        vmem((2, 32, 256), F32),
        vmem((2, 2, 2, 32, 256), BF16),
        vmem((2, 2, 32, 256), BF16),
        pltpu.SemaphoreType.DMA((COPIES,)),
        pltpu.SemaphoreType.DMA((COPIES,)),
    ]
    whole = pl.BlockSpec(memory_space=pltpu.VMEM)
    cell_grad, text_grad = pl.pallas_call(
        kernel,
        out_shape=(
            jax.ShapeDtypeStruct((2, 2, 64, 256), F32),
            jax.ShapeDtypeStruct((64, WIDE), F32),
        ),
        in_specs=[pl.BlockSpec(memory_space=pltpu.HBM)] * 4,
        out_specs=(whole, whole),
        scratch_shapes=scratch,
        compiler_params=pltpu.CompilerParams(
            collective_id=0, has_side_effects=True, vmem_limit_bytes=34 * 1024 * 1024
        ),
    )(
        pltpu.with_memory_space_constraint(cell_states.reshape(2, 2, 64, WIDE), pltpu.HBM),
        pltpu.with_memory_space_constraint(projection, pltpu.HBM),
        pltpu.with_memory_space_constraint(text_embeds, pltpu.HBM),
        pltpu.with_memory_space_constraint(group_ids.reshape(2, 128), pltpu.HBM),
    )
    return cell_grad.reshape(256, 256), text_grad


def solution(mesh):
    return jax.shard_map(
        shards,
        mesh=mesh,
        in_specs=(P("dp", "mp"), P("mp", None), P(("dp", "mp"), None), P("dp")),
        out_specs=(P("dp", "mp"), P(("dp", "mp"), None)),
        check_vma=False,
    )
```
